128 devices in a mesh: src: 8 (over z, y_hi), rcv: 16 (over x, y_lo, core).
Axes of the slice: x: 4, y: 4 (y_hi: 2, y_lo: 2; y = y_hi * 2 + y_lo), z: 4, core: 2. Of those that a mesh axis runs over, the one named last changes fastest.
Arguments:
- records: bfloat16 [512, 512, 512], P('src', 'rcv'), may hold values from -6 to 6
- surface_operator: float32 [256, 2], replicated, may hold values from -0.7 to 0.7
Outputs:
- multiples: bfloat16 [512, 512, 512], P('src', 'rcv')
The draws below stay inside these ranges and needn't reach their ends.
All inputs are finite; a program needn't handle non-finite values.
Results may differ from the reference program's by a relative error of at most 0.011.
Values may be sent and summed in bfloat16 or wider, within the bound.
A program may use at most 64 MiB of HBM per device.

```python
import math
import jax
import jax.numpy as jnp
from jax import lax

NS = 512
NT = 512
NF = 256


def block_scale(own_key, shape, cuts, low, high):
    def one(dim, shards_of):
        steps = jax.random.uniform(jax.random.fold_in(jax.random.fold_in(own_key, 6), dim), (shards_of,), jnp.float32, low / len(cuts), high / len(cuts))
        return jnp.repeat(jnp.exp(steps), shape[dim] // shards_of).reshape((-1,) + (1,) * (len(shape) - dim - 1))

    level = one(*cuts[0])
    for cut in cuts[1:]:
        level = level * one(*cut)
    return level


def centred(key, extent, spread, limit, split=(), dtype=jnp.bfloat16):
    drawn = spread * jax.random.normal(key, extent, jnp.float32)
    if split:
        drawn = drawn * block_scale(key, extent, split, -0.22, 0.18)
    return jnp.clip(drawn, -limit, limit).astype(dtype)


def setup_inputs(seed: int = 0) -> dict:
    splits = jax.random.split(jax.random.key(seed), 3)
    return {
        "records": centred(splits[0], (NS, NS, NT), 1.0, 6.0, ((0, 8), (1, 16))),
        "surface_operator": jnp.clip(jax.random.uniform(splits[1], (NF, 2), jnp.float32, -0.7, 0.7), -0.7, 0.7),
    }


def dft_tables(freqs, samples):
    freq_index = lax.broadcasted_iota(jnp.int32, (freqs, samples), 0)
    time_index = lax.broadcasted_iota(jnp.int32, (freqs, samples), 1)
    phase = (freq_index * time_index % samples).astype(jnp.float32)
    angle = phase * (2.0 * math.pi / samples)
    norming = 1.0 / math.sqrt(samples)
    cosine = jnp.cos(angle) * norming
    sine = jnp.sin(angle) * norming
    weights = jnp.where(freq_index == 0, 1.0, 2.0).astype(jnp.float32)
    forward = jnp.stack([cosine, -sine], axis=1).reshape(2 * freqs, samples)
    inverse = jnp.stack([weights * cosine, -weights * sine], axis=1).reshape(2 * freqs, samples)
    return (forward.astype(jnp.bfloat16), inverse.astype(jnp.bfloat16))

def complex_product(left, right):
    real_part = jnp.dot(left[0], right[0], preferred_element_type=jnp.float32) - jnp.dot(left[1], right[1], preferred_element_type=jnp.float32)
    imag_part = jnp.dot(left[0], right[1], preferred_element_type=jnp.float32) + jnp.dot(left[1], right[0], preferred_element_type=jnp.float32)
    return (real_part, imag_part)

def predict_one(block, coeff):
    recip = (0.5 * (block.astype(jnp.float32) + jnp.swapaxes(block, 1, 2).astype(jnp.float32))).astype(jnp.bfloat16)
    factor = coeff / math.sqrt(NS)

    def scaled(product):
        return jnp.stack([factor[0] * product[0] - factor[1] * product[1], factor[0] * product[1] + factor[1] * product[0]])
    first = scaled(complex_product(recip, recip)).astype(jnp.bfloat16)
    second = scaled(complex_product(recip, first)).astype(jnp.bfloat16)
    third = scaled(complex_product(recip, second))
    return (first.astype(jnp.float32) + second.astype(jnp.float32) + third).astype(jnp.bfloat16)

def reference(records, surface_operator):
    forward, inverse = dft_tables(NF, NT)
    flat_traces = records.reshape(NS * NS, NT)
    spectrum = jnp.dot(forward, flat_traces.T, preferred_element_type=jnp.float32).astype(jnp.bfloat16)
    spectrum = spectrum.reshape(NF, 2, NS, NS)

    def per_freq(pair):
        return predict_one(pair[0], pair[1])
    predicted = lax.map(per_freq, (spectrum, surface_operator))
    result = jnp.dot(predicted.reshape(2 * NF, NS * NS).T, inverse, preferred_element_type=jnp.float32)
    return result.astype(jnp.bfloat16).reshape(NS, NS, NT)
```

```python
import math

import jax
import jax.numpy as jnp
import numpy as np
from jax import lax
from jax.experimental import pallas as pl
from jax.experimental.pallas import tpu as pltpu
from jax.sharding import PartitionSpec as P

MESH = pl.DeviceIdType.MESH
BF = jnp.bfloat16
F32 = jnp.float32
NS = 512
NT = 512
NF = 256
DEV = 128
A = 8
B = 16


def tables():
    f = np.arange(NF)[:, None]
    t = np.arange(NT)[None, :]
    angle = ((f * t) % NT).astype(np.float32) * np.float32(2.0 * math.pi / NT)
    norm = np.float32(1.0 / math.sqrt(NT))
    cosine, sine = np.cos(angle) * norm, np.sin(angle) * norm
    weight = np.where(f == 0, 1.0, 2.0).astype(np.float32)
    forward = np.stack([cosine, -sine], axis=1).reshape(DEV, 2, 2, NT)
    inverse = np.stack([weight * cosine, -weight * sine], axis=1).reshape(DEV, 2, 2, NT)
    forward = forward.transpose(1, 2, 0, 3).reshape(2 * NF, NT)
    inverse = inverse.transpose(1, 0, 2, 3).reshape(2 * NF, NT)
    return forward, inverse


def swap_matrix():
    m = np.zeros((4, 4, 32, 4, 4, 32), np.float32)
    for x in range(4):
        for y in range(4):
            for r in range(32):
                m[x, y, r, y, x, r] = 1.0
    return m.reshape(512, 512)


def far_first():
    rnd = np.random.RandomState(7)
    all_offsets = [(x, y, z, c) for x in range(4) for y in range(4) for z in range(4) for c in range(2)][1:]
    order = rnd.permutation(len(all_offsets))
    shuffled = [all_offsets[i] for i in order]
    return sorted(shuffled, key=lambda o: -sum(min(v, 4 - v) for v in o[:3]))


def nt(left, right):
    return lax.dot_general(left, right, (((1,), (1,)), ((), ())), preferred_element_type=F32)


def nn(left, right):
    return jnp.dot(left, right, preferred_element_type=F32)


def kernel(
    rec, fwd, inv, eye, swap, coef, out,
    wide, slab, rbuf, spec, q_a, b_one, b_two, pred, rslab, rret, gath, turned,
    fs, fr, bs, br, own,
):
    src, rcv = lax.axis_index("src"), lax.axis_index("rcv")
    me = src * B + rcv
    z, y_hi = src // 2, src % 2
    x, y_lo, core = rcv // 4, (rcv // 2) % 2, rcv % 2
    y = y_hi * 2 + y_lo

    barrier = pltpu.get_barrier_semaphore()

    def greet(i, carry):
        to = me ^ i
        pl.semaphore_signal(barrier, inc=1, device_id=(to // B, to % B), device_id_type=MESH)
        return carry

    lax.fori_loop(1, DEV, greet, 0)

    def dft(pair, carry):
        j = 2 * pair
        traces = jnp.concatenate([rec[16 * q + j + jj] for jj in range(2) for q in range(4)], axis=0)
        for h in range(2):
            o = nt(fwd[256 * h : 256 * (h + 1)], traces)
            for c in range(2):
                for jj in range(2):
                    wide[2 * h + c, pl.ds(j + jj, DEV, stride=16), :] = o[
                        128 * c : 128 * (c + 1), 128 * jj : 128 * (jj + 1)
                    ]
        return carry

    lax.fori_loop(0, 8, dft, 0)

    def pack(i, carry):
        for h in range(2):
            for c in range(2):
                v = wide[2 * h + c, pl.ds(i * 256, 256), :]
                slab[h, pl.ds(i * 16, 16), c] = v.astype(BF).reshape(16, 16, 128)
        return carry

    lax.fori_loop(0, 8, pack, 0)

    pl.semaphore_wait(barrier, DEV - 1)

    xs = [lax.rem(x + d, 4) * 4 for d in range(4)]
    ys = [lax.rem(y + d, 4) for d in range(4)]
    y_s = [v // 2 for v in ys]
    y_r = [(v % 2) * 2 for v in ys]
    zs = [lax.rem(z + d, 4) * 2 for d in range(4)]
    cs = [lax.rem(core + d, 2) for d in range(2)]
    peers = [(zs[o[2]] + y_s[o[1]], xs[o[0]] + y_r[o[1]] + cs[o[3]]) for o in far_first()]

    def forward_sends(h, carry):
        mine = pltpu.make_async_copy(slab.at[h, me], rbuf.at[h, src, rcv], fr.at[h])
        mine.start()
        for a, b in peers:
            pltpu.make_async_remote_copy(
                src_ref=slab.at[h, a * B + b],
                dst_ref=rbuf.at[h, src, rcv],
                send_sem=fs.at[h],
                recv_sem=fr.at[h],
                device_id=(a, b),
                device_id_type=MESH,
            ).start()
        return carry

    lax.fori_loop(0, 2, forward_sends, 0)

    norm = 1.0 / math.sqrt(NS)

    def middle(h, carry):
        pltpu.make_async_copy(rbuf.at[h], rbuf.at[h], fr.at[h]).wait()
        for c in range(2):
            for bb in range(4):
                piece = jnp.concatenate(
                    [rbuf[h, :, 4 * bb + k, c].reshape(128, 128) for k in range(4)], axis=1
                )
                s = nn(piece, swap[...]).astype(BF)
                for q in range(4):
                    spec[c, :, q, :, 128 * bb : 128 * (bb + 1)] = s[:, 128 * q : 128 * (q + 1)].reshape(A, 16, 128)
        for c in range(2):
            for m in range(2):
                for n in range(2):
                    turned_s = nt(eye[...], spec[c, 4 * n : 4 * n + 4, :, :, 256 * m : 256 * (m + 1)].reshape(256, 256))
                    plain = spec[c, 4 * m : 4 * m + 4, :, :, 256 * n : 256 * (n + 1)].reshape(256, 256)
                    q = (0.5 * (plain.astype(F32) + turned_s)).astype(BF)
                    rows, cols = slice(256 * m, 256 * (m + 1)), slice(256 * n, 256 * (n + 1))
                    low, right = slice(512 + 256 * m, 768 + 256 * m), slice(512 + 256 * n, 768 + 256 * n)
                    if c == 0:
                        q_a[rows, cols] = q
                        b_one[rows, cols] = q
                        b_one[low, right] = q
                    else:
                        q_a[rows, right] = q
                        b_one[rows, right] = q
                        b_one[low, cols] = -q
        at = 2 * (2 * me + h)
        k_r, k_i = coef[at] * norm, coef[at + 1] * norm

        def scaled(o):
            r, i = o[:, :512], o[:, 512:]
            return k_r * r - k_i * i, k_r * i + k_i * r

        def product(source, target):
            def rows_of(m, carry2):
                at_m = pl.multiple_of(m * 256, 256)
                r, i = scaled(nn(q_a[pl.ds(at_m, 256), :], source[...]))
                r, i = r.astype(BF), i.astype(BF)
                target[pl.ds(at_m, 256), 0:512] = r
                target[pl.ds(at_m, 256), 512:1024] = i
                target[pl.ds(at_m + 512, 256), 0:512] = -i
                target[pl.ds(at_m + 512, 256), 512:1024] = r
                return carry2

            lax.fori_loop(0, 2, rows_of, 0)

        product(b_one, b_two)
        product(b_two, b_one)

        def last(m, carry2):
            at_m = pl.multiple_of(m * 256, 256)
            third = scaled(nn(q_a[pl.ds(at_m, 256), :], b_one[...]))
            for c in range(2):
                cols = slice(512 * c, 512 * (c + 1))
                total = b_two[pl.ds(at_m, 256), cols].astype(F32) + b_one[pl.ds(at_m, 256), cols].astype(F32) + third[c]
                pred[c, pl.ds(m * 4, 4)] = total.astype(BF).reshape(4, 4, 16, 512)
            return carry2

        lax.fori_loop(0, 2, last, 0)

        for c in range(2):
            for bb in range(4):
                piece = jnp.concatenate(
                    [pred[c, :, q, :, 128 * bb : 128 * (bb + 1)].reshape(128, 128) for q in range(4)], axis=1
                )
                s = nn(piece, swap[...]).astype(BF)
                for k in range(4):
                    rslab[h, :, 4 * bb + k, c] = s[:, 128 * k : 128 * (k + 1)].reshape(A, 16, 128)
        mine = pltpu.make_async_copy(rslab.at[h, src, rcv], rret.at[h, me], br.at[h])
        mine.start()
        for a, b in peers:
            pltpu.make_async_remote_copy(
                src_ref=rslab.at[h, a, b],
                dst_ref=rret.at[h, me],
                send_sem=bs.at[h],
                recv_sem=br.at[h],
                device_id=(a, b),
                device_id_type=MESH,
            ).start()
        return carry

    lax.fori_loop(0, 2, middle, 0)

    def gather(h, carry):
        pltpu.make_async_copy(rret.at[h], rret.at[h], br.at[h]).wait()

        def widen(i, carry2):
            gath[pl.ds(pl.multiple_of(i * 512, 512), 512), :] = rret[h, pl.ds(i * 16, 16)].reshape(512, 128).astype(F32)
            return carry2

        lax.fori_loop(0, 8, widen, 0)

        def turn(j, carry2):
            w = gath[pl.ds(j, 256, stride=16), :].astype(BF)
            turned[h, pl.ds(pl.multiple_of(j * 128, 128), 128), :] = nt(eye[0:128, 0:128], w).astype(BF)
            return carry2

        lax.fori_loop(0, 16, turn, 0)
        return carry

    lax.fori_loop(0, 2, gather, 0)

    def inverse(pair, carry):
        at = pl.multiple_of(pair * 256, 256)
        o = nn(turned[0, pl.ds(at, 256), :], inv[0:256, :]) + nn(turned[1, pl.ds(at, 256), :], inv[256:512, :])
        o = o.astype(BF)
        for jj in range(2):
            for q in range(4):
                out[16 * q + 2 * pair + jj] = o[128 * jj + 32 * q : 128 * jj + 32 * (q + 1), :]
        return carry

    lax.fori_loop(0, 8, inverse, 0)

    whole = pl.ds(0, DEV - 1)
    for h in range(2):
        pltpu.make_async_copy(slab.at[h, whole], slab.at[h, whole], fs.at[h]).wait()
        pltpu.make_async_copy(rret.at[h, whole], rret.at[h, whole], bs.at[h]).wait()


def local(records, surface_operator):
    forward, inverse = tables()
    consts = [jnp.asarray(v).astype(BF) for v in (forward, inverse, np.eye(256, dtype=np.float32), swap_matrix())]
    vmem = pl.BlockSpec(memory_space=pltpu.VMEM)
    return pl.pallas_call(
        kernel,
        name="multiples",
        out_shape=jax.ShapeDtypeStruct((64, 32, NT), BF),
        in_specs=[vmem] * 5 + [pl.BlockSpec(memory_space=pltpu.SMEM)],
        out_specs=vmem,
        scratch_shapes=[
            pltpu.VMEM((4, 2048, 128), F32),
            pltpu.VMEM((2, DEV, 2, 16, 128), BF),
            pltpu.VMEM((2, A, B, 2, 16, 128), BF),
            pltpu.VMEM((2, A, 4, 16, 512), BF),
            pltpu.VMEM((512, 1024), BF),
            pltpu.VMEM((1024, 1024), BF),
            pltpu.VMEM((1024, 1024), BF),
            pltpu.VMEM((2, A, 4, 16, 512), BF),
            pltpu.VMEM((2, A, B, 2, 16, 128), BF),
            pltpu.VMEM((2, DEV, 2, 16, 128), BF),
            pltpu.VMEM((4096, 128), F32),
            pltpu.VMEM((2, 2048, 256), BF),
            pltpu.SemaphoreType.DMA((2,)),
            pltpu.SemaphoreType.DMA((2,)),
            pltpu.SemaphoreType.DMA((2,)),
            pltpu.SemaphoreType.DMA((2,)),
            pltpu.SemaphoreType.DMA((2,)),
        ],
        compiler_params=pltpu.CompilerParams(
            collective_id=0, has_side_effects=True, vmem_limit_bytes=56 * 1024 * 1024
        ),
    )(records, *consts, surface_operator.reshape(2 * NF))


def solution(mesh):
    placed = (P("src", "rcv", None), P())
    return jax.shard_map(
        local, mesh=mesh, in_specs=placed, out_specs=P("src", "rcv", None), check_vma=False
    )
```

```python
import math

import jax
import jax.numpy as jnp
import numpy as np
from jax import lax
from jax.experimental import pallas as pl
from jax.experimental.pallas import tpu as pltpu
from jax.sharding import PartitionSpec as P

MESH = pl.DeviceIdType.MESH
BF = jnp.bfloat16
F32 = jnp.float32
NS = 512
NT = 512
NF = 256
DEV = 128
A = 8
B = 16


def tables():
    f = np.arange(NF)[:, None]
    t = np.arange(NT)[None, :]
    angle = ((f * t) % NT).astype(np.float32) * np.float32(2.0 * math.pi / NT)
    norm = np.float32(1.0 / math.sqrt(NT))
    cosine, sine = np.cos(angle) * norm, np.sin(angle) * norm
    weight = np.where(f == 0, 1.0, 2.0).astype(np.float32)
    forward = np.stack([cosine, -sine], axis=1).reshape(DEV, 2, 2, NT)
    inverse = np.stack([weight * cosine, -weight * sine], axis=1).reshape(DEV, 2, 2, NT)
    forward = forward.transpose(1, 2, 0, 3).reshape(2 * NF, NT)
    inverse = inverse.transpose(1, 0, 2, 3).reshape(2 * NF, NT)
    return forward, inverse


def swap_matrix():
    m = np.zeros((4, 4, 32, 4, 4, 32), np.float32)
    for x in range(4):
        for y in range(4):
            for r in range(32):
                m[x, y, r, y, x, r] = 1.0
    return m.reshape(512, 512)


def far_first():
    rnd = np.random.RandomState(7)
    all_offsets = [(x, y, z, c) for x in range(4) for y in range(4) for z in range(4) for c in range(2)][1:]
    order = rnd.permutation(len(all_offsets))
    shuffled = [all_offsets[i] for i in order]
    return sorted(shuffled, key=lambda o: -sum(min(v, 4 - v) for v in o[:3]))


def nt(left, right):
    return lax.dot_general(left, right, (((1,), (1,)), ((), ())), preferred_element_type=F32)


def nn(left, right):
    return jnp.dot(left, right, preferred_element_type=F32)


def kernel(
    rec_in, tab_in, coef, out,
    rec, fwd, inv, eye, swap,
    wide, slab, rbuf, spec, q_a, b_one, b_two, pred, rslab, rret, gath, turned,
    fs, fr, bs, br, loaded,
):
    def tab(i):
        return tab_in.at[pl.ds(512 * i, 512)]

    loads = [
        pltpu.make_async_copy(here, there, loaded.at[i])
        for i, (here, there) in enumerate(
            [(tab(0), fwd), (rec_in, rec), (tab(2), swap), (tab_in.at[pl.ds(1536, 256), pl.ds(0, 256)], eye), (tab(1), inv)]
        )
    ]
    for load in loads:
        load.start()
    src, rcv = lax.axis_index("src"), lax.axis_index("rcv")
    me = src * B + rcv
    z, y_hi = src // 2, src % 2
    x, y_lo, core = rcv // 4, (rcv // 2) % 2, rcv % 2
    y = y_hi * 2 + y_lo

    barrier = pltpu.get_barrier_semaphore()

    xs = [lax.rem(x + d, 4) * 4 for d in range(4)]
    ys = [lax.rem(y + d, 4) for d in range(4)]
    y_s = [v // 2 for v in ys]
    y_r = [(v % 2) * 2 for v in ys]
    zs = [lax.rem(z + d, 4) * 2 for d in range(4)]
    cs = [lax.rem(core + d, 2) for d in range(2)]
    peers = [(zs[o[2]] + y_s[o[1]], xs[o[0]] + y_r[o[1]] + cs[o[3]]) for o in far_first()]
    for to in peers:
        pl.semaphore_signal(barrier, inc=1, device_id=to, device_id_type=MESH)
    loads[0].wait()
    loads[1].wait()

    def dft(h):
        def step(pair, carry):
            j = 2 * pair
            traces = jnp.concatenate([rec[16 * q + j + jj] for jj in range(2) for q in range(4)], axis=0)
            o = nt(fwd[256 * h : 256 * (h + 1)], traces)
            for c in range(2):
                for jj in range(2):
                    wide[c, pl.ds(j + jj, DEV, stride=16), :] = o[
                        128 * c : 128 * (c + 1), 128 * jj : 128 * (jj + 1)
                    ]
            return carry

        lax.fori_loop(0, 8, step, 0, unroll=4)

        def pack(i, carry):
            for c in range(2):
                v = wide[c, pl.ds(i * 256, 256), :]
                slab[h, pl.ds(i * 16, 16), c] = v.astype(BF).reshape(16, 16, 128)
            return carry

        lax.fori_loop(0, 8, pack, 0, unroll=2)

    def forward_sends(h):
        mine = pltpu.make_async_copy(slab.at[h, me], rbuf.at[h, src, rcv], fr.at[h])
        mine.start()
        for a, b in peers:
            pltpu.make_async_remote_copy(
                src_ref=slab.at[h, a * B + b],
                dst_ref=rbuf.at[h, src, rcv],
                send_sem=fs.at[h],
                recv_sem=fr.at[h],
                device_id=(a, b),
                device_id_type=MESH,
            ).start()

    dft(0)
    pl.semaphore_wait(barrier, DEV - 1)
    forward_sends(0)
    dft(1)
    forward_sends(1)
    loads[2].wait()
    loads[3].wait()

    norm = 1.0 / math.sqrt(NS)

    def middle(h, carry):
        pltpu.make_async_copy(rbuf.at[h], rbuf.at[h], fr.at[h]).wait()
        for c in range(2):
            for bb in range(4):
                piece = jnp.concatenate(
                    [rbuf[h, :, 4 * bb + k, c].reshape(128, 128) for k in range(4)], axis=1
                )
                s = nn(piece, swap[...]).astype(BF)
                for q in range(4):
                    spec[c, :, q, :, 128 * bb : 128 * (bb + 1)] = s[:, 128 * q : 128 * (q + 1)].reshape(A, 16, 128)
        for c in range(2):
            for m in range(2):
                for n in range(2):
                    turned_s = nt(eye[...], spec[c, 4 * n : 4 * n + 4, :, :, 256 * m : 256 * (m + 1)].reshape(256, 256))
                    plain = spec[c, 4 * m : 4 * m + 4, :, :, 256 * n : 256 * (n + 1)].reshape(256, 256)
                    q = (0.5 * (plain.astype(F32) + turned_s)).astype(BF)
                    rows, cols = slice(256 * m, 256 * (m + 1)), slice(256 * n, 256 * (n + 1))
                    low, right = slice(512 + 256 * m, 768 + 256 * m), slice(512 + 256 * n, 768 + 256 * n)
                    if c == 0:
                        q_a[rows, cols] = q
                        b_one[rows, cols] = q
                        b_one[low, right] = q
                    else:
                        q_a[rows, right] = q
                        b_one[rows, right] = q
                        b_one[low, cols] = -q
        at = 2 * me + h
        k_r, k_i = coef[0, at] * norm, coef[1, at] * norm

        def scaled(o):
            r, i = o[:, :512], o[:, 512:]
            return k_r * r - k_i * i, k_r * i + k_i * r

        def product(source, target):
            def rows_of(m, carry2):
                at_m = pl.multiple_of(m * 256, 256)
                r, i = scaled(nn(q_a[pl.ds(at_m, 256), :], source[...]))
                r, i = r.astype(BF), i.astype(BF)
                target[pl.ds(at_m, 256), 0:512] = r
                target[pl.ds(at_m, 256), 512:1024] = i
                target[pl.ds(at_m + 512, 256), 0:512] = -i
                target[pl.ds(at_m + 512, 256), 512:1024] = r
                return carry2

            lax.fori_loop(0, 2, rows_of, 0)

        product(b_one, b_two)
        product(b_two, b_one)

        def last(m, carry2):
            at_m = pl.multiple_of(m * 256, 256)
            third = scaled(nn(q_a[pl.ds(at_m, 256), :], b_one[...]))
            for c in range(2):
                cols = slice(512 * c, 512 * (c + 1))
                total = b_two[pl.ds(at_m, 256), cols].astype(F32) + b_one[pl.ds(at_m, 256), cols].astype(F32) + third[c]
                pred[c, pl.ds(m * 4, 4)] = total.astype(BF).reshape(4, 4, 16, 512)
            return carry2

        lax.fori_loop(0, 2, last, 0)

        for c in range(2):
            for bb in range(4):
                piece = jnp.concatenate(
                    [pred[c, :, q, :, 128 * bb : 128 * (bb + 1)].reshape(128, 128) for q in range(4)], axis=1
                )
                s = nn(piece, swap[...]).astype(BF)
                for k in range(4):
                    rslab[h, :, 4 * bb + k, c] = s[:, 128 * k : 128 * (k + 1)].reshape(A, 16, 128)
        mine = pltpu.make_async_copy(rslab.at[h, src, rcv], rret.at[h, me], br.at[h])
        mine.start()
        for a, b in peers:
            pltpu.make_async_remote_copy(
                src_ref=rslab.at[h, a, b],
                dst_ref=rret.at[h, me],
                send_sem=bs.at[h],
                recv_sem=br.at[h],
                device_id=(a, b),
                device_id_type=MESH,
            ).start()
        return carry

    lax.fori_loop(0, 2, middle, 0)

    def gather(h, carry):
        pltpu.make_async_copy(rret.at[h], rret.at[h], br.at[h]).wait()

        def widen(i, carry2):
            gath[pl.ds(pl.multiple_of(i * 512, 512), 512), :] = rret[h, pl.ds(i * 16, 16)].reshape(512, 128).astype(F32)
            return carry2

        lax.fori_loop(0, 8, widen, 0, unroll=2)

        def turn(j, carry2):
            w = gath[pl.ds(j, 256, stride=16), :].astype(BF)
            turned[h, pl.ds(pl.multiple_of(j * 128, 128), 128), :] = nt(eye[0:128, 0:128], w).astype(BF)
            return carry2

        lax.fori_loop(0, 16, turn, 0, unroll=8)
        return carry

    lax.fori_loop(0, 2, gather, 0)

    loads[4].wait()

    def inverse(pair, carry):
        at = pl.multiple_of(pair * 256, 256)
        o = nn(turned[0, pl.ds(at, 256), :], inv[0:256, :]) + nn(turned[1, pl.ds(at, 256), :], inv[256:512, :])
        o = o.astype(BF)
        for jj in range(2):
            for q in range(4):
                out[16 * q + 2 * pair + jj] = o[128 * jj + 32 * q : 128 * jj + 32 * (q + 1), :]
        return carry

    lax.fori_loop(0, 8, inverse, 0, unroll=4)

    whole = pl.ds(0, DEV - 1)
    for h in range(2):
        pltpu.make_async_copy(slab.at[h, whole], slab.at[h, whole], fs.at[h]).wait()
        pltpu.make_async_copy(rret.at[h, whole], rret.at[h, whole], bs.at[h]).wait()


def local(records, surface_operator):
    forward, inverse = tables()
    packed = np.concatenate([forward, inverse, swap_matrix(), np.eye(768, 512, dtype=np.float32)])
    vmem = pl.BlockSpec(memory_space=pltpu.VMEM)
    return pl.pallas_call(
        kernel,
        name="multiples",
        out_shape=jax.ShapeDtypeStruct((64, 32, NT), BF),
        in_specs=[pl.BlockSpec(memory_space=pl.ANY)] * 2 + [pl.BlockSpec(memory_space=pltpu.SMEM)],
        out_specs=vmem,
        scratch_shapes=[
            pltpu.VMEM((64, 32, NT), BF),
            pltpu.VMEM((2 * NF, NT), BF),
            pltpu.VMEM((2 * NF, NT), BF),
            pltpu.VMEM((256, 256), BF),
            pltpu.VMEM((512, 512), BF),
            pltpu.VMEM((2, 2048, 128), F32),
            pltpu.VMEM((2, DEV, 2, 16, 128), BF),
            pltpu.VMEM((2, A, B, 2, 16, 128), BF),
            pltpu.VMEM((2, A, 4, 16, 512), BF),
            pltpu.VMEM((512, 1024), BF),
            pltpu.VMEM((1024, 1024), BF),
            pltpu.VMEM((1024, 1024), BF),
            pltpu.VMEM((2, A, 4, 16, 512), BF),
            pltpu.VMEM((2, A, B, 2, 16, 128), BF),
            pltpu.VMEM((2, DEV, 2, 16, 128), BF),
            pltpu.VMEM((4096, 128), F32),
            pltpu.VMEM((2, 2048, 256), BF),
            pltpu.SemaphoreType.DMA((2,)),
            pltpu.SemaphoreType.DMA((2,)),
            pltpu.SemaphoreType.DMA((2,)),
            pltpu.SemaphoreType.DMA((2,)),
            pltpu.SemaphoreType.DMA((5,)),
        ],
        compiler_params=pltpu.CompilerParams(
            collective_id=0, has_side_effects=True, vmem_limit_bytes=50 * 1024 * 1024 + 512 * 1024
        ),
    )(records, jnp.asarray(packed).astype(BF), surface_operator.T)


def solution(mesh):
    placed = (P("src", "rcv", None), P())
    return jax.shard_map(
        local, mesh=mesh, in_specs=placed, out_specs=P("src", "rcv", None), check_vma=False
    )
```

```python
import math

import jax
import jax.numpy as jnp
import numpy as np
from jax import lax
from jax.experimental import pallas as pl
from jax.experimental.pallas import tpu as pltpu
from jax.sharding import PartitionSpec as P

MESH = pl.DeviceIdType.MESH
BF = jnp.bfloat16
F32 = jnp.float32
NS = 512
NT = 512
NF = 256
DEV = 128
A = 8
B = 16


def tables():
    f = np.arange(NF)[:, None]
    t = np.arange(NT)[None, :]
    angle = ((f * t) % NT).astype(np.float32) * np.float32(2.0 * math.pi / NT)
    norm = np.float32(1.0 / math.sqrt(NT))
    cosine, sine = np.cos(angle) * norm, np.sin(angle) * norm
    weight = np.where(f == 0, 1.0, 2.0).astype(np.float32)
    forward = np.stack([cosine, -sine], axis=1).reshape(DEV, 2, 2, NT)
    inverse = np.stack([weight * cosine, -weight * sine], axis=1).reshape(DEV, 2, 2, NT)
    forward = forward.transpose(1, 2, 0, 3).reshape(2 * NF, NT)
    inverse = inverse.reshape(A, 4, 4, 2, 2, NT).transpose(1, 3, 0, 2, 4, 5).reshape(2 * NF, NT)
    return forward, inverse


def swap_matrix():
    m = np.zeros((4, 4, 32, 4, 4, 32), np.float32)
    for x in range(4):
        for y in range(4):
            for r in range(32):
                m[x, y, r, y, x, r] = 1.0
    return m.reshape(512, 512)


def mixed_offsets():
    offsets = [(x, y, z, c) for x in range(4) for y in range(4) for z in range(4) for c in range(2)][1:]
    return [offsets[i] for i in np.random.RandomState(1).permutation(len(offsets))]


RETURN_ORDER = (2, 0, 1, 3)


def nt(left, right):
    return lax.dot_general(left, right, (((1,), (1,)), ((), ())), preferred_element_type=F32)


def nn(left, right):
    return jnp.dot(left, right, preferred_element_type=F32)


def kernel(
    rec_in, tab_in, coef_in, out,
    rec, fwd, inv, eye, swap, coef,
    wide, slab, rbuf, spec, q_a, b_one, b_two, rslab, rret, gath, turned, total,
    fs, fr, bs, br, loaded, filled,
):
    def tab(i):
        return tab_in.at[pl.ds(512 * i, 512)]

    loads = [
        pltpu.make_async_copy(here, there, loaded.at[i])
        for i, (here, there) in enumerate(
            [(tab(0), fwd), (tab(2), swap), (tab_in.at[pl.ds(1536, 256), pl.ds(0, 256)], eye), (coef_in, coef)]
        )
    ]
    loads[0].start()
    for part in range(4):
        for q in range(4):
            some = pl.ds(16 * q + 4 * part, 4)
            pltpu.make_async_copy(rec_in.at[some], rec.at[some], filled.at[part]).start()
    for load in loads[1:]:
        load.start()
    src, rcv = lax.axis_index("src"), lax.axis_index("rcv")
    me = src * B + rcv
    z, y_hi = src // 2, src % 2
    x, y_lo, core = rcv // 4, (rcv // 2) % 2, rcv % 2
    y = y_hi * 2 + y_lo

    barrier = pltpu.get_barrier_semaphore()

    xs = [lax.rem(x + d, 4) * 4 for d in range(4)]
    ys = [lax.rem(y + d, 4) for d in range(4)]
    y_s = [v // 2 for v in ys]
    y_r = [(v % 2) * 2 for v in ys]
    zs = [lax.rem(z + d, 4) * 2 for d in range(4)]
    cs = [lax.rem(core + d, 2) for d in range(2)]
    offsets = mixed_offsets()
    peers = [(zs[o[2]] + y_s[o[1]], xs[o[0]] + y_r[o[1]] + cs[o[3]]) for o in offsets]
    for _, to in sorted(zip(offsets, peers, strict=True), key=lambda p: -sum(min(v, 4 - v) for v in p[0][:3])):
        pl.semaphore_signal(barrier, inc=1, device_id=to, device_id_type=MESH)
    loads[0].wait()

    def dft(h):
        def step(pair, carry):
            j = 2 * pair
            traces = jnp.concatenate([rec[16 * q + j + jj] for jj in range(2) for q in range(4)], axis=0)
            o = nt(fwd[256 * h : 256 * (h + 1)], traces)
            for c in range(2):
                for jj in range(2):
                    wide[c, pl.ds(j + jj, DEV, stride=16), :] = o[
                        128 * c : 128 * (c + 1), 128 * jj : 128 * (jj + 1)
                    ]
            return carry

        if h == 0:
            for part in range(4):
                pltpu.make_async_copy(rec.at[pl.ds(0, 16)], rec.at[pl.ds(0, 16)], filled.at[part]).wait()
                for pair in range(2):
                    step(2 * part + pair, 0)
        else:
            lax.fori_loop(0, 8, step, 0, unroll=4)

        def pack(i, carry):
            for c in range(2):
                v = wide[c, pl.ds(i * 256, 256), :]
                slab[h, pl.ds(i * 16, 16), c] = v.astype(BF).reshape(16, 16, 128)
            return carry

        lax.fori_loop(0, 8, pack, 0, unroll=2)

    def forward_sends(h):
        mine = pltpu.make_async_copy(slab.at[h, me], rbuf.at[h, src, rcv], fr.at[h])
        mine.start()
        for a, b in peers:
            pltpu.make_async_remote_copy(
                src_ref=slab.at[h, a * B + b],
                dst_ref=rbuf.at[h, src, rcv],
                send_sem=fs.at[h],
                recv_sem=fr.at[h],
                device_id=(a, b),
                device_id_type=MESH,
            ).start()

    dft(0)
    pl.semaphore_wait(barrier, DEV - 1)
    forward_sends(0)
    dft(1)
    forward_sends(1)
    for h in range(2):
        for p, d in enumerate(RETURN_ORDER):
            at = pl.multiple_of((lax.rem(x + 4 - d, 4) * 2 + h) * 64 + 512, 64)
            pltpu.make_async_copy(
                tab_in.at[pl.ds(at, 64)], inv.at[pl.ds(256 * h + 64 * p, 64)], filled.at[4]
            ).start()
    for load in loads[1:]:
        load.wait()
    pltpu.make_async_copy(inv, inv, filled.at[4]).wait()

    norm = 1.0 / math.sqrt(NS)

    def middle(h, carry):
        pltpu.make_async_copy(rbuf.at[h], rbuf.at[h], fr.at[h]).wait()
        for c in range(2):
            piece = jnp.concatenate(
                [
                    jnp.concatenate([rbuf[h, :, 4 * bb + k, c].reshape(128, 128) for k in range(4)], axis=1)
                    for bb in range(4)
                ],
                axis=0,
            )
            s = nn(piece, swap[...]).astype(BF)
            for bb in range(4):
                for q in range(4):
                    spec[c, :, q, :, 128 * bb : 128 * (bb + 1)] = s[
                        128 * bb : 128 * (bb + 1), 128 * q : 128 * (q + 1)
                    ].reshape(A, 16, 128)
        for c in range(2):
            for m in range(2):
                for n in range(2):
                    turned_s = nt(eye[...], spec[c, 4 * n : 4 * n + 4, :, :, 256 * m : 256 * (m + 1)].reshape(256, 256))
                    plain = spec[c, 4 * m : 4 * m + 4, :, :, 256 * n : 256 * (n + 1)].reshape(256, 256)
                    q = (0.5 * (plain.astype(F32) + turned_s)).astype(BF)
                    rows, cols = slice(256 * m, 256 * (m + 1)), slice(256 * n, 256 * (n + 1))
                    low, right = slice(512 + 256 * m, 768 + 256 * m), slice(512 + 256 * n, 768 + 256 * n)
                    if c == 0:
                        q_a[rows, cols] = q
                        b_one[rows, cols] = q
                        b_one[low, right] = q
                    else:
                        q_a[rows, right] = q
                        b_one[rows, right] = q
                        b_one[low, cols] = -q
        at = 2 * me + h
        k_r, k_i = coef[0, at] * norm, coef[1, at] * norm

        def scaled(o):
            half = o.shape[1] // 2
            r, i = o[:, :half], o[:, half:]
            return k_r * r - k_i * i, k_r * i + k_i * r

        def product(source, target):
            def rows_of(m, carry2):
                at_m = pl.multiple_of(m * 256, 256)
                r, i = scaled(nn(q_a[pl.ds(at_m, 256), :], source[...]))
                r, i = r.astype(BF), i.astype(BF)
                target[pl.ds(at_m, 256), 0:512] = r
                target[pl.ds(at_m, 256), 512:1024] = i
                target[pl.ds(at_m + 512, 256), 0:512] = -i
                target[pl.ds(at_m + 512, 256), 512:1024] = r
                return carry2

            lax.fori_loop(0, 2, rows_of, 0)

        product(b_one, b_two)
        product(b_two, b_one)

        for p, d in enumerate(RETURN_ORDER):
            bb = lax.rem(x + d, 4)
            cols = [pl.ds(pl.multiple_of(512 * c + 128 * bb, 128), 128) for c in range(2)]
            third = scaled(nn(q_a[...], jnp.concatenate([b_one[:, cols[0]], b_one[:, cols[1]]], axis=1)))
            pieces = []
            for c in range(2):
                summed = b_two[0:512, cols[c]].astype(F32) + b_one[0:512, cols[c]].astype(F32) + third[c]
                summed = summed.astype(BF).reshape(A, 4, 16, 128)
                pieces.append(jnp.concatenate([summed[:, q].reshape(128, 128) for q in range(4)], axis=1))
            s = nn(jnp.concatenate(pieces, axis=0), swap[...]).astype(BF)
            for c in range(2):
                for k in range(4):
                    rslab[h, :, 4 * bb + k, c] = s[128 * c : 128 * (c + 1), 128 * k : 128 * (k + 1)].reshape(A, 16, 128)
            if p % 2 == 0:
                continue
            for e in RETURN_ORDER[p - 1 : p + 1]:
                there = rret.at[h, RETURN_ORDER.index(e), src * 4 + rcv % 4]
                if e == 0:
                    pltpu.make_async_copy(rslab.at[h, src, rcv], there, br.at[h, p // 2]).start()
            for o, (a, b) in zip(offsets, peers, strict=True):
                if o[0] in RETURN_ORDER[p - 1 : p + 1]:
                    pltpu.make_async_remote_copy(
                        src_ref=rslab.at[h, a, b],
                        dst_ref=rret.at[h, RETURN_ORDER.index(o[0]), src * 4 + rcv % 4],
                        send_sem=bs.at[h],
                        recv_sem=br.at[h, p // 2],
                        device_id=(a, b),
                        device_id_type=MESH,
                    ).start()
        return carry

    lax.fori_loop(0, 2, middle, 0)

    def gather(h, pair):
        pltpu.make_async_copy(
            rret.at[h, pl.ds(2 * pair, 2)], rret.at[h, pl.ds(2 * pair, 2)], br.at[h, pair]
        ).wait()
        for i in range(8):
            v = rret[h, 2 * pair + i // 4, 8 * (i % 4) : 8 * (i % 4 + 1)]
            gath[256 * i : 256 * (i + 1), :] = v.reshape(256, 128).astype(F32)

        def turn(j, carry):
            w = gath[pl.ds(j, 128, stride=16), :].astype(BF)
            turned[h, pl.ds(pl.multiple_of(j * 128, 128), 128), 128 * pair : 128 * (pair + 1)] = nt(
                eye[0:128, 0:128], w
            ).astype(BF)
            return carry

        lax.fori_loop(0, 16, turn, 0, unroll=8)

    gather(0, 0)
    gather(0, 1)

    def first_half(i, carry):
        at = pl.ds(pl.multiple_of(i * 256, 256), 256)
        total[at, :] = nn(turned[0, at, :], inv[0:256, :])
        return carry

    lax.fori_loop(0, 8, first_half, 0, unroll=4)
    gather(1, 0)
    gather(1, 1)

    def inverse(pair, carry):
        at = pl.ds(pl.multiple_of(pair * 256, 256), 256)
        o = (total[at, :] + nn(turned[1, at, :], inv[256:512, :])).astype(BF)
        for jj in range(2):
            for q in range(4):
                out[16 * q + 2 * pair + jj] = o[128 * jj + 32 * q : 128 * jj + 32 * (q + 1), :]
        return carry

    lax.fori_loop(0, 8, inverse, 0, unroll=4)

    whole = pl.ds(0, DEV - 1)
    for h in range(2):
        pltpu.make_async_copy(slab.at[h, whole], slab.at[h, whole], fs.at[h]).wait()
        pltpu.make_async_copy(slab.at[h, whole], slab.at[h, whole], bs.at[h]).wait()


def local(records, surface_operator):
    forward, inverse = tables()
    packed = np.concatenate([forward, inverse, swap_matrix(), np.eye(768, 512, dtype=np.float32)])
    vmem = pl.BlockSpec(memory_space=pltpu.VMEM)
    return pl.pallas_call(
        kernel,
        name="multiples",
        out_shape=jax.ShapeDtypeStruct((64, 32, NT), BF),
        in_specs=[pl.BlockSpec(memory_space=pl.ANY)] * 3,
        out_specs=vmem,
        scratch_shapes=[
            pltpu.VMEM((64, 32, NT), BF),
            pltpu.VMEM((2 * NF, NT), BF),
            pltpu.VMEM((2 * NF, NT), BF),
            pltpu.VMEM((256, 256), BF),
            pltpu.VMEM((512, 512), BF),
            pltpu.SMEM((2, NF), F32),
            pltpu.VMEM((2, 2048, 128), F32),
            pltpu.VMEM((2, DEV, 2, 16, 128), BF),
            pltpu.VMEM((2, A, B, 2, 16, 128), BF),
            pltpu.VMEM((2, A, 4, 16, 512), BF),
            pltpu.VMEM((512, 1024), BF),
            pltpu.VMEM((1024, 1024), BF),
            pltpu.VMEM((1024, 1024), BF),
            pltpu.VMEM((2, A, B, 2, 16, 128), BF),
            pltpu.VMEM((2, 4, 32, 2, 16, 128), BF),
            pltpu.VMEM((2048, 128), F32),
            pltpu.VMEM((2, 2048, 256), BF),
            pltpu.VMEM((2048, NT), F32),
            pltpu.SemaphoreType.DMA((2,)),
            pltpu.SemaphoreType.DMA((2,)),
            pltpu.SemaphoreType.DMA((2,)),
            pltpu.SemaphoreType.DMA((2, 2)),
            pltpu.SemaphoreType.DMA((4,)),
            pltpu.SemaphoreType.DMA((5,)),
        ],
        compiler_params=pltpu.CompilerParams(
            collective_id=0, has_side_effects=True, vmem_limit_bytes=50 * 1024 * 1024 + 512 * 1024
        ),
    )(records, jnp.asarray(packed).astype(BF), surface_operator.T)


def solution(mesh):
    placed = (P("src", "rcv", None), P())
    return jax.shard_map(
        local, mesh=mesh, in_specs=placed, out_specs=P("src", "rcv", None), check_vma=False
    )
```

```python
import math

import jax
import jax.numpy as jnp
import numpy as np
from jax import lax
from jax.experimental import pallas as pl
from jax.experimental.pallas import tpu as pltpu
from jax.sharding import PartitionSpec as P

MESH = pl.DeviceIdType.MESH
BF = jnp.bfloat16
F32 = jnp.float32
NS = 512
NT = 512
NF = 256
DEV = 128
A = 8
B = 16


def tables():
    f = np.arange(NF)[:, None]
    t = np.arange(NT)[None, :]
    angle = ((f * t) % NT).astype(np.float32) * np.float32(2.0 * math.pi / NT)
    norm = np.float32(1.0 / math.sqrt(NT))
    cosine, sine = np.cos(angle) * norm, np.sin(angle) * norm
    weight = np.where(f == 0, 1.0, 2.0).astype(np.float32)
    forward = np.stack([cosine, -sine], axis=1).reshape(DEV, 2, 2, NT)
    inverse = np.stack([weight * cosine, -weight * sine], axis=1).reshape(DEV, 2, 2, NT)
    forward = forward.transpose(1, 2, 0, 3).reshape(2 * NF, NT)
    inverse = inverse.reshape(A, 4, 4, 2, 2, NT).transpose(1, 3, 0, 2, 4, 5).reshape(2 * NF, NT)
    return forward, inverse


def swap_matrix():
    m = np.zeros((4, 4, 32, 4, 4, 32), np.float32)
    for x in range(4):
        for y in range(4):
            for r in range(32):
                m[x, y, r, y, x, r] = 1.0
    return m.reshape(512, 512)


def mixed_offsets():
    offsets = [(x, y, z, c) for x in range(4) for y in range(4) for z in range(4) for c in range(2)][1:]
    return [offsets[i] for i in np.random.RandomState(1).permutation(len(offsets))]


RETURN_ORDER = (2, 0, 1, 3)


def nt(left, right):
    return lax.dot_general(left, right, (((1,), (1,)), ((), ())), preferred_element_type=F32)


def nn(left, right):
    return jnp.dot(left, right, preferred_element_type=F32)


def kernel(
    rec_in, tab_in, coef_in, total, late, inv_late,
    rec, fwd, inv_early, eye, swap, coef,
    wide, slab, rbuf, spec, q_a, b_one, b_two, rslab, rret, gath, early,
    fs, fr, bs, br, loaded, filled,
):
    def tab(i):
        return tab_in.at[pl.ds(512 * i, 512)]

    loads = [
        pltpu.make_async_copy(here, there, loaded.at[i])
        for i, (here, there) in enumerate(
            [(tab(0), fwd), (tab(2), swap), (tab_in.at[pl.ds(1536, 256), pl.ds(0, 256)], eye), (coef_in, coef)]
        )
    ]
    loads[0].start()
    for part in range(4):
        for q in range(4):
            some = pl.ds(16 * q + 4 * part, 4)
            pltpu.make_async_copy(rec_in.at[some], rec.at[some], filled.at[part]).start()
    for load in loads[1:]:
        load.start()
    src, rcv = lax.axis_index("src"), lax.axis_index("rcv")
    me = src * B + rcv
    z, y_hi = src // 2, src % 2
    x, y_lo, core = rcv // 4, (rcv // 2) % 2, rcv % 2
    y = y_hi * 2 + y_lo

    barrier = pltpu.get_barrier_semaphore()

    xs = [lax.rem(x + d, 4) * 4 for d in range(4)]
    ys = [lax.rem(y + d, 4) for d in range(4)]
    y_s = [v // 2 for v in ys]
    y_r = [(v % 2) * 2 for v in ys]
    zs = [lax.rem(z + d, 4) * 2 for d in range(4)]
    cs = [lax.rem(core + d, 2) for d in range(2)]
    offsets = mixed_offsets()
    peers = [(zs[o[2]] + y_s[o[1]], xs[o[0]] + y_r[o[1]] + cs[o[3]]) for o in offsets]
    for _, to in sorted(zip(offsets, peers, strict=True), key=lambda p: -sum(min(v, 4 - v) for v in p[0][:3])):
        pl.semaphore_signal(barrier, inc=1, device_id=to, device_id_type=MESH)
    loads[0].wait()

    def dft(h):
        def step(pair, carry):
            j = 2 * pair
            traces = jnp.concatenate([rec[16 * q + j + jj] for jj in range(2) for q in range(4)], axis=0)
            o = nt(fwd[256 * h : 256 * (h + 1)], traces)
            for c in range(2):
                for jj in range(2):
                    wide[c, pl.ds(j + jj, DEV, stride=16), :] = o[
                        128 * c : 128 * (c + 1), 128 * jj : 128 * (jj + 1)
                    ]
            return carry

        if h == 0:
            for part in range(4):
                pltpu.make_async_copy(rec.at[pl.ds(0, 16)], rec.at[pl.ds(0, 16)], filled.at[part]).wait()
        lax.fori_loop(0, 8, step, 0, unroll=8)

        def pack(i, carry):
            for c in range(2):
                v = wide[c, pl.ds(i * 256, 256), :]
                slab[h, pl.ds(i * 16, 16), c] = v.astype(BF).reshape(16, 16, 128)
            return carry

        lax.fori_loop(0, 8, pack, 0, unroll=2)

    def forward_sends(h):
        mine = pltpu.make_async_copy(slab.at[h, me], rbuf.at[h, src, rcv], fr.at[h])
        mine.start()
        for _, (a, b) in sorted(zip(offsets, peers, strict=True), key=lambda p: -sum(min(v, 4 - v) for v in p[0][:3])) if h == 0 else zip(offsets, peers, strict=True):
            pltpu.make_async_remote_copy(
                src_ref=slab.at[h, a * B + b],
                dst_ref=rbuf.at[h, src, rcv],
                send_sem=fs.at[h],
                recv_sem=fr.at[h],
                device_id=(a, b),
                device_id_type=MESH,
            ).start()

    dft(0)
    pl.semaphore_wait(barrier, DEV - 1)
    forward_sends(0)
    dft(1)
    forward_sends(1)
    for h in range(2):
        for p, d in enumerate(RETURN_ORDER):
            at = pl.multiple_of((lax.rem(x + 4 - d, 4) * 2 + h) * 64 + 512, 64)
            pltpu.make_async_copy(
                tab_in.at[pl.ds(at, 64)], (inv_late if h else inv_early).at[pl.ds(64 * p, 64)], filled.at[4 + h]
            ).start()
    for load in loads[1:]:
        load.wait()
    pltpu.make_async_copy(inv_early, inv_early, filled.at[4]).wait()
    pltpu.make_async_copy(inv_late, inv_late, filled.at[5]).wait()

    norm = 1.0 / math.sqrt(NS)

    def middle(h, carry):
        pltpu.make_async_copy(rbuf.at[h], rbuf.at[h], fr.at[h]).wait()
        for c in range(2):
            piece = jnp.concatenate(
                [
                    jnp.concatenate([rbuf[h, :, 4 * bb + k, c].reshape(128, 128) for k in range(4)], axis=1)
                    for bb in range(4)
                ],
                axis=0,
            )
            s = nn(piece, swap[...]).astype(BF)
            for bb in range(4):
                for q in range(4):
                    spec[c, :, q, :, 128 * bb : 128 * (bb + 1)] = s[
                        128 * bb : 128 * (bb + 1), 128 * q : 128 * (q + 1)
                    ].reshape(A, 16, 128)
        for c in range(2):
            for m in range(2):
                for n in range(2):
                    turned_s = nt(eye[...], spec[c, 4 * n : 4 * n + 4, :, :, 256 * m : 256 * (m + 1)].reshape(256, 256))
                    plain = spec[c, 4 * m : 4 * m + 4, :, :, 256 * n : 256 * (n + 1)].reshape(256, 256)
                    q = (0.5 * (plain.astype(F32) + turned_s)).astype(BF)
                    rows, cols = slice(256 * m, 256 * (m + 1)), slice(256 * n, 256 * (n + 1))
                    low, right = slice(512 + 256 * m, 768 + 256 * m), slice(512 + 256 * n, 768 + 256 * n)
                    if c == 0:
                        q_a[rows, cols] = q
                        b_one[rows, cols] = q
                        b_one[low, right] = q
                    else:
                        q_a[rows, right] = q
                        b_one[rows, right] = q
                        b_one[low, cols] = -q
        at = 2 * me + h
        k_r, k_i = coef[0, at] * norm, coef[1, at] * norm

        def scaled(o):
            half = o.shape[1] // 2
            r, i = o[:, :half], o[:, half:]
            return k_r * r - k_i * i, k_r * i + k_i * r

        def product(source, target):
            def rows_of(m, carry2):
                at_m = pl.multiple_of(m * 256, 256)
                r, i = scaled(nn(q_a[pl.ds(at_m, 256), :], source[...]))
                r, i = r.astype(BF), i.astype(BF)
                target[pl.ds(at_m, 256), 0:512] = r
                target[pl.ds(at_m, 256), 512:1024] = i
                target[pl.ds(at_m + 512, 256), 0:512] = -i
                target[pl.ds(at_m + 512, 256), 512:1024] = r
                return carry2

            lax.fori_loop(0, 2, rows_of, 0)

        product(b_one, b_two)
        product(b_two, b_one)

        for p, d in enumerate(RETURN_ORDER):
            bb = lax.rem(x + d, 4)
            cols = [pl.ds(pl.multiple_of(512 * c + 128 * bb, 128), 128) for c in range(2)]
            third = scaled(nn(q_a[...], jnp.concatenate([b_one[:, cols[0]], b_one[:, cols[1]]], axis=1)))
            pieces = []
            for c in range(2):
                summed = b_two[0:512, cols[c]].astype(F32) + b_one[0:512, cols[c]].astype(F32) + third[c]
                summed = summed.astype(BF).reshape(A, 4, 16, 128)
                pieces.append(jnp.concatenate([summed[:, q].reshape(128, 128) for q in range(4)], axis=1))
            s = nn(jnp.concatenate(pieces, axis=0), swap[...]).astype(BF)
            for c in range(2):
                for k in range(4):
                    rslab[h, :, 4 * bb + k, c] = s[128 * c : 128 * (c + 1), 128 * k : 128 * (k + 1)].reshape(A, 16, 128)
            if p % 2 == 0:
                continue
            for e in RETURN_ORDER[p - 1 : p + 1]:
                there = rret.at[h, RETURN_ORDER.index(e), src * 4 + rcv % 4]
                if e == 0:
                    pltpu.make_async_copy(rslab.at[h, src, rcv], there, br.at[h, p // 2]).start()
            for o, (a, b) in sorted(zip(offsets, peers, strict=True), key=lambda p: -sum(min(v, 4 - v) for v in p[0][:3])):
                if o[0] in RETURN_ORDER[p - 1 : p + 1]:
                    pltpu.make_async_remote_copy(
                        src_ref=rslab.at[h, a, b],
                        dst_ref=rret.at[h, RETURN_ORDER.index(o[0]), src * 4 + rcv % 4],
                        send_sem=bs.at[h],
                        recv_sem=br.at[h, p // 2],
                        device_id=(a, b),
                        device_id_type=MESH,
                    ).start()
        return carry

    lax.fori_loop(0, 2, middle, 0)

    def gather(h, pair, turned):
        pltpu.make_async_copy(
            rret.at[h, pl.ds(2 * pair, 2)], rret.at[h, pl.ds(2 * pair, 2)], br.at[h, pair]
        ).wait()
        for i in range(8):
            v = rret[h, 2 * pair + i // 4, 8 * (i % 4) : 8 * (i % 4 + 1)]
            gath[256 * i : 256 * (i + 1), :] = v.reshape(256, 128).astype(F32)

        def turn(j, carry):
            w = gath[pl.ds(j, 128, stride=16), :].astype(BF)
            turned[pl.ds(pl.multiple_of(j * 128, 128), 128), 128 * pair : 128 * (pair + 1)] = nt(
                eye[0:128, 0:128], w
            ).astype(BF)
            return carry

        lax.fori_loop(0, 16, turn, 0, unroll=8)

    gather(0, 0, early)
    gather(0, 1, early)

    def first_half(i, carry):
        at = pl.ds(pl.multiple_of(i * 256, 256), 256)
        total[at, :] = nn(early[at, :], inv_early[...])
        return carry

    lax.fori_loop(0, 8, first_half, 0, unroll=4)
    gather(1, 0, late)
    gather(1, 1, late)

    whole = pl.ds(0, DEV - 1)
    for h in range(2):
        pltpu.make_async_copy(slab.at[h, whole], slab.at[h, whole], fs.at[h]).wait()
        pltpu.make_async_copy(slab.at[h, whole], slab.at[h, whole], bs.at[h]).wait()


def finish(total, late, inv_late, out, done, sem):
    copies = []
    for i in range(8):
        at = slice(256 * i, 256 * (i + 1))
        o = (total[at, :] + nn(late[at, :], inv_late[...])).astype(BF).reshape(2, 4, 32, NT)
        for jj in range(2):
            done[:, 2 * i + jj] = o[jj]
        copies.append(pltpu.make_async_copy(done.at[:, pl.ds(2 * i, 2)], out.at[:, pl.ds(2 * i, 2)], sem.at[i]))
        copies[-1].start()
    for copy in copies:
        copy.wait()


def local(records, surface_operator):
    forward, inverse = tables()
    packed = np.concatenate([forward, inverse, swap_matrix(), np.eye(256, 512, dtype=np.float32)])
    packed = jnp.asarray(packed).astype(BF)
    vmem = pl.BlockSpec(memory_space=pltpu.VMEM)
    total, late, inv_late = pl.pallas_call(
        kernel,
        name="multiples",
        out_shape=[
            jax.ShapeDtypeStruct((2048, NT), F32),
            jax.ShapeDtypeStruct((2048, NF), BF),
            jax.ShapeDtypeStruct((NF, NT), BF),
        ],
        in_specs=[pl.BlockSpec(memory_space=pl.ANY)] * 3,
        out_specs=[vmem] * 3,
        scratch_shapes=[
            pltpu.VMEM((64, 32, NT), BF),
            pltpu.VMEM((2 * NF, NT), BF),
            pltpu.VMEM((NF, NT), BF),
            pltpu.VMEM((256, 256), BF),
            pltpu.VMEM((512, 512), BF),
            pltpu.SMEM((2, NF), F32),
            pltpu.VMEM((2, 2048, 128), F32),
            pltpu.VMEM((2, DEV, 2, 16, 128), BF),
            pltpu.VMEM((2, A, B, 2, 16, 128), BF),
            pltpu.VMEM((2, A, 4, 16, 512), BF),
            pltpu.VMEM((512, 1024), BF),
            pltpu.VMEM((1024, 1024), BF),
            pltpu.VMEM((1024, 1024), BF),
            pltpu.VMEM((2, A, B, 2, 16, 128), BF),
            pltpu.VMEM((2, 4, 32, 2, 16, 128), BF),
            pltpu.VMEM((2048, 128), F32),
            pltpu.VMEM((2048, NF), BF),
            pltpu.SemaphoreType.DMA((2,)),
            pltpu.SemaphoreType.DMA((2,)),
            pltpu.SemaphoreType.DMA((2,)),
            pltpu.SemaphoreType.DMA((2, 2)),
            pltpu.SemaphoreType.DMA((4,)),
            pltpu.SemaphoreType.DMA((6,)),
        ],
        compiler_params=pltpu.CompilerParams(
            collective_id=0, has_side_effects=True, vmem_limit_bytes=40 * 1024 * 1024
        ),
    )(*[pltpu.with_memory_space_constraint(v, pltpu.HBM) for v in (records, packed, surface_operator.T)])
    multiples = pl.pallas_call(
        finish,
        name="finish",
        out_shape=jax.ShapeDtypeStruct((4, 16, 32, NT), BF),
        in_specs=[vmem] * 3,
        out_specs=pl.BlockSpec(memory_space=pl.ANY),
        scratch_shapes=[pltpu.VMEM((4, 16, 32, NT), BF), pltpu.SemaphoreType.DMA((8,))],
        compiler_params=pltpu.CompilerParams(vmem_limit_bytes=16 * 1024 * 1024),
    )(total, late, inv_late)
    return multiples.reshape(64, 32, NT)


def solution(mesh):
    placed = (P("src", "rcv", None), P())
    return jax.shard_map(
        local, mesh=mesh, in_specs=placed, out_specs=P("src", "rcv", None), check_vma=False
    )
```

```python
import math

import jax
import jax.numpy as jnp
import numpy as np
from jax import lax
from jax.experimental import pallas as pl
from jax.experimental.pallas import tpu as pltpu
from jax.sharding import PartitionSpec as P

MESH = pl.DeviceIdType.MESH
BF = jnp.bfloat16
F32 = jnp.float32
NS = 512
NT = 512
NF = 256
DEV = 128
A = 8
B = 16


def tables():
    f = np.arange(NF)[:, None]
    t = np.arange(NT)[None, :]
    angle = ((f * t) % NT).astype(np.float32) * np.float32(2.0 * math.pi / NT)
    norm = np.float32(1.0 / math.sqrt(NT))
    cosine, sine = np.cos(angle) * norm, np.sin(angle) * norm
    weight = np.where(f == 0, 1.0, 2.0).astype(np.float32)
    forward = np.stack([cosine, -sine], axis=1).reshape(DEV, 2, 2, NT)
    inverse = np.stack([weight * cosine, -weight * sine], axis=1).reshape(DEV, 2, 2, NT)
    forward = forward.transpose(1, 2, 0, 3).reshape(2 * NF, NT)
    inverse = inverse.reshape(A, 4, 4, 2, 2, NT).transpose(1, 3, 0, 2, 4, 5).reshape(2 * NF, NT)
    return forward, inverse


def swap_matrix():
    m = np.zeros((4, 4, 32, 4, 4, 32), np.float32)
    for x in range(4):
        for y in range(4):
            for r in range(32):
                m[x, y, r, y, x, r] = 1.0
    return m.reshape(512, 512)


def mixed_offsets():
    offsets = [(x, y, z, c) for x in range(4) for y in range(4) for z in range(4) for c in range(2)][1:]
    return [offsets[i] for i in np.random.RandomState(1).permutation(len(offsets))]


RETURN_ORDER = (2, 1, 0, 3)


def nt(left, right):
    return lax.dot_general(left, right, (((1,), (1,)), ((), ())), preferred_element_type=F32)


def nn(left, right):
    return jnp.dot(left, right, preferred_element_type=F32)


def kernel(
    rec_in, tab_in, coef_in, total, late, inv_late,
    rec, fwd, inv_early, eye, swap, coef,
    wide, slab, rbuf, spec, q_a, b_one, b_two, rslab, rret, gath, early,
    fs, fr, bs, br, loaded, filled,
):
    def tab(i):
        return tab_in.at[pl.ds(512 * i, 512)]

    loads = [
        pltpu.make_async_copy(here, there, loaded.at[i])
        for i, (here, there) in enumerate(
            [(tab(0), fwd), (tab(2), swap), (tab_in.at[pl.ds(1536, 256), pl.ds(0, 256)], eye), (coef_in, coef)]
        )
    ]
    loads[0].start()
    for part in range(4):
        for q in range(4):
            some = pl.ds(16 * q + 4 * part, 4)
            pltpu.make_async_copy(rec_in.at[some], rec.at[some], filled.at[part]).start()
    for load in loads[1:]:
        load.start()
    src, rcv = lax.axis_index("src"), lax.axis_index("rcv")
    me = src * B + rcv
    z, y_hi = src // 2, src % 2
    x, y_lo, core = rcv // 4, (rcv // 2) % 2, rcv % 2
    y = y_hi * 2 + y_lo

    barrier = pltpu.get_barrier_semaphore()

    xs = [lax.rem(x + d, 4) * 4 for d in range(4)]
    ys = [lax.rem(y + d, 4) for d in range(4)]
    y_s = [v // 2 for v in ys]
    y_r = [(v % 2) * 2 for v in ys]
    zs = [lax.rem(z + d, 4) * 2 for d in range(4)]
    cs = [lax.rem(core + d, 2) for d in range(2)]
    offsets = mixed_offsets()
    peers = [(zs[o[2]] + y_s[o[1]], xs[o[0]] + y_r[o[1]] + cs[o[3]]) for o in offsets]
    for _, to in sorted(zip(offsets, peers, strict=True), key=lambda p: -sum(min(v, 4 - v) for v in p[0][:3])):
        pl.semaphore_signal(barrier, inc=1, device_id=to, device_id_type=MESH)
    loads[0].wait()

    def dft(h):
        def step(pair, carry):
            j = 2 * pair
            traces = jnp.concatenate([rec[16 * q + j + jj] for jj in range(2) for q in range(4)], axis=0)
            o = nt(fwd[256 * h : 256 * (h + 1)], traces)
            for c in range(2):
                for jj in range(2):
                    wide[c, pl.ds(j + jj, DEV, stride=16), :] = o[
                        128 * c : 128 * (c + 1), 128 * jj : 128 * (jj + 1)
                    ]
            return carry

        if h == 0:
            for part in range(4):
                pltpu.make_async_copy(rec.at[pl.ds(0, 16)], rec.at[pl.ds(0, 16)], filled.at[part]).wait()
        lax.fori_loop(0, 8, step, 0, unroll=8)

        def pack(i, carry):
            for c in range(2):
                v = wide[c, pl.ds(i * 256, 256), :]
                slab[h, pl.ds(i * 16, 16), c] = v.astype(BF).reshape(16, 16, 128)
            return carry

        lax.fori_loop(0, 8, pack, 0, unroll=2)

    def forward_sends(h):
        mine = pltpu.make_async_copy(slab.at[h, me], rbuf.at[h, src, rcv], fr.at[h])
        mine.start()
        for _, (a, b) in sorted(zip(offsets, peers, strict=True), key=lambda p: -sum(min(v, 4 - v) for v in p[0][:3])) if h == 0 else zip(offsets, peers, strict=True):
            pltpu.make_async_remote_copy(
                src_ref=slab.at[h, a * B + b],
                dst_ref=rbuf.at[h, src, rcv],
                send_sem=fs.at[h],
                recv_sem=fr.at[h],
                device_id=(a, b),
                device_id_type=MESH,
            ).start()

    dft(0)
    pl.semaphore_wait(barrier, DEV - 1)
    forward_sends(0)
    dft(1)
    forward_sends(1)
    for h in range(2):
        for p, d in enumerate(RETURN_ORDER):
            at = pl.multiple_of((lax.rem(x + 4 - d, 4) * 2 + h) * 64 + 512, 64)
            pltpu.make_async_copy(
                tab_in.at[pl.ds(at, 64)], (inv_late if h else inv_early).at[pl.ds(64 * p, 64)], filled.at[4 + h]
            ).start()
    for load in loads[1:]:
        load.wait()
    pltpu.make_async_copy(inv_early, inv_early, filled.at[4]).wait()
    pltpu.make_async_copy(inv_late, inv_late, filled.at[5]).wait()

    norm = 1.0 / math.sqrt(NS)

    def middle(h, carry):
        pltpu.make_async_copy(rbuf.at[h], rbuf.at[h], fr.at[h]).wait()
        for c in range(2):
            piece = jnp.concatenate(
                [
                    jnp.concatenate([rbuf[h, :, 4 * bb + k, c].reshape(128, 128) for k in range(4)], axis=1)
                    for bb in range(4)
                ],
                axis=0,
            )
            s = nn(piece, swap[...]).astype(BF)
            for bb in range(4):
                for q in range(4):
                    spec[c, :, q, :, 128 * bb : 128 * (bb + 1)] = s[
                        128 * bb : 128 * (bb + 1), 128 * q : 128 * (q + 1)
                    ].reshape(A, 16, 128)
        for c in range(2):
            for m in range(2):
                for n in range(2):
                    turned_s = nt(eye[...], spec[c, 4 * n : 4 * n + 4, :, :, 256 * m : 256 * (m + 1)].reshape(256, 256))
                    plain = spec[c, 4 * m : 4 * m + 4, :, :, 256 * n : 256 * (n + 1)].reshape(256, 256)
                    q = (0.5 * (plain.astype(F32) + turned_s)).astype(BF)
                    rows, cols = slice(256 * m, 256 * (m + 1)), slice(256 * n, 256 * (n + 1))
                    low, right = slice(512 + 256 * m, 768 + 256 * m), slice(512 + 256 * n, 768 + 256 * n)
                    if c == 0:
                        q_a[rows, cols] = q
                        b_one[rows, cols] = q
                        b_one[low, right] = q
                    else:
                        q_a[rows, right] = q
                        b_one[rows, right] = q
                        b_one[low, cols] = -q
        at = 2 * me + h
        k_r, k_i = coef[0, at] * norm, coef[1, at] * norm

        def scaled(o):
            half = o.shape[1] // 2
            r, i = o[:, :half], o[:, half:]
            return k_r * r - k_i * i, k_r * i + k_i * r

        def product(source, target):
            def rows_of(m, carry2):
                at_m = pl.multiple_of(m * 256, 256)
                r, i = scaled(nn(q_a[pl.ds(at_m, 256), :], source[...]))
                r, i = r.astype(BF), i.astype(BF)
                target[pl.ds(at_m, 256), 0:512] = r
                target[pl.ds(at_m, 256), 512:1024] = i
                target[pl.ds(at_m + 512, 256), 0:512] = -i
                target[pl.ds(at_m + 512, 256), 512:1024] = r
                return carry2

            lax.fori_loop(0, 2, rows_of, 0)

        product(b_one, b_two)
        product(b_two, b_one)

        for p, d in enumerate(RETURN_ORDER):
            bb = lax.rem(x + d, 4)
            cols = [pl.ds(pl.multiple_of(512 * c + 128 * bb, 128), 128) for c in range(2)]
            third = scaled(nn(q_a[...], jnp.concatenate([b_one[:, cols[0]], b_one[:, cols[1]]], axis=1)))
            pieces = []
            for c in range(2):
                summed = b_two[0:512, cols[c]].astype(F32) + b_one[0:512, cols[c]].astype(F32) + third[c]
                summed = summed.astype(BF).reshape(A, 4, 16, 128)
                pieces.append(jnp.concatenate([summed[:, q].reshape(128, 128) for q in range(4)], axis=1))
            s = nn(jnp.concatenate(pieces, axis=0), swap[...]).astype(BF)
            for c in range(2):
                for k in range(4):
                    rslab[h, :, 4 * bb + k, c] = s[128 * c : 128 * (c + 1), 128 * k : 128 * (k + 1)].reshape(A, 16, 128)
            if p % 2 == 0:
                continue
            for e in RETURN_ORDER[p - 1 : p + 1]:
                there = rret.at[h, RETURN_ORDER.index(e), src * 4 + rcv % 4]
                if e == 0:
                    pltpu.make_async_copy(rslab.at[h, src, rcv], there, br.at[h, p // 2]).start()
            for o, (a, b) in sorted(zip(offsets, peers, strict=True), key=lambda p: -sum(min(v, 4 - v) for v in p[0][:3])):
                if o[0] in RETURN_ORDER[p - 1 : p + 1]:
                    pltpu.make_async_remote_copy(
                        src_ref=rslab.at[h, a, b],
                        dst_ref=rret.at[h, RETURN_ORDER.index(o[0]), src * 4 + rcv % 4],
                        send_sem=bs.at[h],
                        recv_sem=br.at[h, p // 2],
                        device_id=(a, b),
                        device_id_type=MESH,
                    ).start()
        return carry

    lax.fori_loop(0, 2, middle, 0)

    def gather(h, pair, turned):
        pltpu.make_async_copy(
            rret.at[h, pl.ds(2 * pair, 2)], rret.at[h, pl.ds(2 * pair, 2)], br.at[h, pair]
        ).wait()
        for i in range(8):
            v = rret[h, 2 * pair + i // 4, 8 * (i % 4) : 8 * (i % 4 + 1)]
            gath[256 * i : 256 * (i + 1), :] = v.reshape(256, 128).astype(F32)

        def turn(j, carry):
            w = gath[pl.ds(j, 128, stride=16), :].astype(BF)
            turned[pl.ds(pl.multiple_of(j * 128, 128), 128), 128 * pair : 128 * (pair + 1)] = nt(
                eye[0:128, 0:128], w
            ).astype(BF)
            return carry

        lax.fori_loop(0, 16, turn, 0, unroll=8)

    gather(0, 0, early)
    gather(0, 1, early)

    def first_half(i, carry):
        at = pl.ds(pl.multiple_of(i * 256, 256), 256)
        total[at, :] = nn(early[at, :], inv_early[...])
        return carry

    lax.fori_loop(0, 8, first_half, 0, unroll=4)
    gather(1, 0, late)
    gather(1, 1, late)

    whole = pl.ds(0, DEV - 1)
    for h in range(2):
        pltpu.make_async_copy(slab.at[h, whole], slab.at[h, whole], fs.at[h]).wait()
        pltpu.make_async_copy(slab.at[h, whole], slab.at[h, whole], bs.at[h]).wait()


def finish(total, late, inv_late, out, done, sem):
    copies = []
    for i in range(8):
        at = slice(256 * i, 256 * (i + 1))
        o = (total[at, :] + nn(late[at, :], inv_late[...])).astype(BF).reshape(2, 4, 32, NT)
        for jj in range(2):
            done[:, 2 * i + jj] = o[jj]
        copies.append(pltpu.make_async_copy(done.at[:, pl.ds(2 * i, 2)], out.at[:, pl.ds(2 * i, 2)], sem.at[i]))
        copies[-1].start()
    for copy in copies:
        copy.wait()


def local(records, surface_operator):
    forward, inverse = tables()
    packed = np.concatenate([forward, inverse, swap_matrix(), np.eye(256, 512, dtype=np.float32)])
    packed = jnp.asarray(packed).astype(BF)
    vmem = pl.BlockSpec(memory_space=pltpu.VMEM)
    total, late, inv_late = pl.pallas_call(
        kernel,
        name="multiples",
        out_shape=[
            jax.ShapeDtypeStruct((2048, NT), F32),
            jax.ShapeDtypeStruct((2048, NF), BF),
            jax.ShapeDtypeStruct((NF, NT), BF),
        ],
        in_specs=[pl.BlockSpec(memory_space=pl.ANY)] * 3,
        out_specs=[vmem] * 3,
        scratch_shapes=[
            pltpu.VMEM((64, 32, NT), BF),
            pltpu.VMEM((2 * NF, NT), BF),
            pltpu.VMEM((NF, NT), BF),
            pltpu.VMEM((256, 256), BF),
            pltpu.VMEM((512, 512), BF),
            pltpu.SMEM((2, NF), F32),
            pltpu.VMEM((2, 2048, 128), F32),
            pltpu.VMEM((2, DEV, 2, 16, 128), BF),
            pltpu.VMEM((2, A, B, 2, 16, 128), BF),
            pltpu.VMEM((2, A, 4, 16, 512), BF),
            pltpu.VMEM((512, 1024), BF),
            pltpu.VMEM((1024, 1024), BF),
            pltpu.VMEM((1024, 1024), BF),
            pltpu.VMEM((2, A, B, 2, 16, 128), BF),
            pltpu.VMEM((2, 4, 32, 2, 16, 128), BF),
            pltpu.VMEM((2048, 128), F32),
            pltpu.VMEM((2048, NF), BF),
            pltpu.SemaphoreType.DMA((2,)),
            pltpu.SemaphoreType.DMA((2,)),
            pltpu.SemaphoreType.DMA((2,)),
            pltpu.SemaphoreType.DMA((2, 2)),
            pltpu.SemaphoreType.DMA((4,)),
            pltpu.SemaphoreType.DMA((6,)),
        ],
        compiler_params=pltpu.CompilerParams(
            collective_id=0, has_side_effects=True, vmem_limit_bytes=40 * 1024 * 1024
        ),
    )(*[pltpu.with_memory_space_constraint(v, pltpu.HBM) for v in (records, packed, surface_operator.T)])
    multiples = pl.pallas_call(
        finish,
        name="finish",
        out_shape=jax.ShapeDtypeStruct((4, 16, 32, NT), BF),
        in_specs=[vmem] * 3,
        out_specs=pl.BlockSpec(memory_space=pl.ANY),
        scratch_shapes=[pltpu.VMEM((4, 16, 32, NT), BF), pltpu.SemaphoreType.DMA((8,))],
        compiler_params=pltpu.CompilerParams(vmem_limit_bytes=16 * 1024 * 1024),
    )(total, late, inv_late)
    return multiples.reshape(64, 32, NT)


def solution(mesh):
    placed = (P("src", "rcv", None), P())
    return jax.shard_map(
        local, mesh=mesh, in_specs=placed, out_specs=P("src", "rcv", None), check_vma=False
    )
```

```python
import math

import jax
import jax.numpy as jnp
import numpy as np
from jax import lax
from jax.experimental import pallas as pl
from jax.experimental.pallas import tpu as pltpu
from jax.sharding import PartitionSpec as P

MESH = pl.DeviceIdType.MESH
BF = jnp.bfloat16
F32 = jnp.float32
NS = 512
NT = 512
NF = 256
DEV = 128
A = 8
B = 16


def tables():
    f = np.arange(NF)[:, None]
    t = np.arange(NT)[None, :]
    angle = ((f * t) % NT).astype(np.float32) * np.float32(2.0 * math.pi / NT)
    norm = np.float32(1.0 / math.sqrt(NT))
    cosine, sine = np.cos(angle) * norm, np.sin(angle) * norm
    weight = np.where(f == 0, 1.0, 2.0).astype(np.float32)
    forward = np.stack([cosine, -sine], axis=1).reshape(DEV, 2, 2, NT)
    inverse = np.stack([weight * cosine, -weight * sine], axis=1).reshape(DEV, 2, 2, NT)
    forward = forward.transpose(1, 2, 0, 3).reshape(2 * NF, NT)
    inverse = inverse.reshape(A, 4, 4, 2, 2, NT).transpose(1, 3, 0, 2, 4, 5).reshape(2 * NF, NT)
    return forward, inverse


def swap_matrix():
    m = np.zeros((4, 4, 32, 4, 4, 32), np.float32)
    for x in range(4):
        for y in range(4):
            for r in range(32):
                m[x, y, r, y, x, r] = 1.0
    return m.reshape(512, 512)


def mixed_offsets():
    offsets = [(x, y, z, c) for x in range(4) for y in range(4) for z in range(4) for c in range(2)][1:]
    return [offsets[i] for i in np.random.RandomState(1).permutation(len(offsets))]


RETURN_ORDER = (2, 1, 0, 3)


def nt(left, right):
    return lax.dot_general(left, right, (((1,), (1,)), ((), ())), preferred_element_type=F32)


def nn(left, right):
    return jnp.dot(left, right, preferred_element_type=F32)


def kernel(
    rec_in, tab_in, coef_in, total, late, inv_late,
    rec, fwd, inv_early, eye, swap, coef,
    wide, slab, rbuf, spec, q_a, b_one, b_two, rslab, rret, gath, early,
    fs, fr, bs, br, loaded, filled,
):
    def tab(i):
        return tab_in.at[pl.ds(512 * i, 512)]

    loads = [
        pltpu.make_async_copy(here, there, loaded.at[i])
        for i, (here, there) in enumerate(
            [(tab(0), fwd), (tab(2), swap), (tab_in.at[pl.ds(1536, 256), pl.ds(0, 256)], eye), (coef_in, coef)]
        )
    ]
    loads[0].start()
    traces_in = pltpu.make_async_copy(rec_in, rec, filled.at[0])
    traces_in.start()
    src, rcv = lax.axis_index("src"), lax.axis_index("rcv")
    me = src * B + rcv
    z, y_hi = src // 2, src % 2
    x, y_lo, core = rcv // 4, (rcv // 2) % 2, rcv % 2
    y = y_hi * 2 + y_lo

    barrier = pltpu.get_barrier_semaphore()

    xs = [lax.rem(x + d, 4) * 4 for d in range(4)]
    ys = [lax.rem(y + d, 4) for d in range(4)]
    y_s = [v // 2 for v in ys]
    y_r = [(v % 2) * 2 for v in ys]
    zs = [lax.rem(z + d, 4) * 2 for d in range(4)]
    cs = [lax.rem(core + d, 2) for d in range(2)]
    offsets = mixed_offsets()
    peers = [(zs[o[2]] + y_s[o[1]], xs[o[0]] + y_r[o[1]] + cs[o[3]]) for o in offsets]
    for _, to in sorted(zip(offsets, peers, strict=True), key=lambda p: -sum(min(v, 4 - v) for v in p[0][:3])):
        pl.semaphore_signal(barrier, inc=1, device_id=to, device_id_type=MESH)
    for load in loads[1:]:
        load.start()
    loads[0].wait()
    traces_in.wait()

    def dft(h):
        def step(pair, carry):
            j = 2 * pair
            traces = jnp.concatenate([rec[16 * q + j + jj] for jj in range(2) for q in range(4)], axis=0)
            o = nt(fwd[256 * h : 256 * (h + 1)], traces)
            for c in range(2):
                for jj in range(2):
                    wide[c, pl.ds(j + jj, DEV, stride=16), :] = o[
                        128 * c : 128 * (c + 1), 128 * jj : 128 * (jj + 1)
                    ]
            return carry

        lax.fori_loop(0, 8, step, 0, unroll=8)

        def pack(i, carry):
            for c in range(2):
                v = wide[c, pl.ds(i * 256, 256), :]
                slab[h, pl.ds(i * 16, 16), c] = v.astype(BF).reshape(16, 16, 128)
            return carry

        lax.fori_loop(0, 8, pack, 0, unroll=4)

    def forward_sends(h):
        mine = pltpu.make_async_copy(slab.at[h, me], rbuf.at[h, src, rcv], fr.at[h])
        mine.start()
        for _, (a, b) in sorted(zip(offsets, peers, strict=True), key=lambda p: -sum(min(v, 4 - v) for v in p[0][:3])) if h == 0 else zip(offsets, peers, strict=True):
            pltpu.make_async_remote_copy(
                src_ref=slab.at[h, a * B + b],
                dst_ref=rbuf.at[h, src, rcv],
                send_sem=fs.at[h],
                recv_sem=fr.at[h],
                device_id=(a, b),
                device_id_type=MESH,
            ).start()

    dft(0)
    pl.semaphore_wait(barrier, DEV - 1)
    forward_sends(0)
    dft(1)
    forward_sends(1)
    for h in range(2):
        for p, d in enumerate(RETURN_ORDER):
            at = pl.multiple_of((lax.rem(x + 4 - d, 4) * 2 + h) * 64 + 512, 64)
            pltpu.make_async_copy(
                tab_in.at[pl.ds(at, 64)], (inv_late if h else inv_early).at[pl.ds(64 * p, 64)], filled.at[1 + h]
            ).start()
    for load in loads[1:]:
        load.wait()
    pltpu.make_async_copy(inv_early, inv_early, filled.at[1]).wait()
    pltpu.make_async_copy(inv_late, inv_late, filled.at[2]).wait()

    norm = 1.0 / math.sqrt(NS)

    def middle(h, carry):
        pltpu.make_async_copy(rbuf.at[h], rbuf.at[h], fr.at[h]).wait()
        for c in range(2):
            piece = jnp.concatenate(
                [
                    jnp.concatenate([rbuf[h, :, 4 * bb + k, c].reshape(128, 128) for k in range(4)], axis=1)
                    for bb in range(4)
                ],
                axis=0,
            )
            s = nn(piece, swap[...]).astype(BF)
            for bb in range(4):
                for q in range(4):
                    spec[c, :, q, :, 128 * bb : 128 * (bb + 1)] = s[
                        128 * bb : 128 * (bb + 1), 128 * q : 128 * (q + 1)
                    ].reshape(A, 16, 128)
        for c in range(2):
            for m in range(2):
                for n in range(2):
                    turned_s = nt(eye[...], spec[c, 4 * n : 4 * n + 4, :, :, 256 * m : 256 * (m + 1)].reshape(256, 256))
                    plain = spec[c, 4 * m : 4 * m + 4, :, :, 256 * n : 256 * (n + 1)].reshape(256, 256)
                    q = (0.5 * (plain.astype(F32) + turned_s)).astype(BF)
                    rows, cols = slice(256 * m, 256 * (m + 1)), slice(256 * n, 256 * (n + 1))
                    low, right = slice(512 + 256 * m, 768 + 256 * m), slice(512 + 256 * n, 768 + 256 * n)
                    if c == 0:
                        q_a[rows, cols] = q
                        b_one[rows, cols] = q
                        b_one[low, right] = q
                    else:
                        q_a[rows, right] = q
                        b_one[rows, right] = q
                        b_one[low, cols] = -q
        at = 2 * me + h
        k_r, k_i = coef[0, at] * norm, coef[1, at] * norm

        def scaled(o):
            half = o.shape[1] // 2
            r, i = o[:, :half], o[:, half:]
            return k_r * r - k_i * i, k_r * i + k_i * r

        def product(source, target):
            def rows_of(m, carry2):
                at_m = pl.multiple_of(m * 256, 256)
                r, i = scaled(nn(q_a[pl.ds(at_m, 256), :], source[...]))
                r, i = r.astype(BF), i.astype(BF)
                target[pl.ds(at_m, 256), 0:512] = r
                target[pl.ds(at_m, 256), 512:1024] = i
                target[pl.ds(at_m + 512, 256), 0:512] = -i
                target[pl.ds(at_m + 512, 256), 512:1024] = r
                return carry2

            lax.fori_loop(0, 2, rows_of, 0)

        product(b_one, b_two)
        product(b_two, b_one)

        for p, d in enumerate(RETURN_ORDER):
            bb = lax.rem(x + d, 4)
            cols = [pl.ds(pl.multiple_of(512 * c + 128 * bb, 128), 128) for c in range(2)]
            third = scaled(nn(q_a[...], jnp.concatenate([b_one[:, cols[0]], b_one[:, cols[1]]], axis=1)))
            pieces = []
            for c in range(2):
                summed = b_two[0:512, cols[c]].astype(F32) + b_one[0:512, cols[c]].astype(F32) + third[c]
                summed = summed.astype(BF).reshape(A, 4, 16, 128)
                pieces.append(jnp.concatenate([summed[:, q].reshape(128, 128) for q in range(4)], axis=1))
            s = nn(jnp.concatenate(pieces, axis=0), swap[...]).astype(BF)
            for c in range(2):
                for k in range(4):
                    rslab[h, :, 4 * bb + k, c] = s[128 * c : 128 * (c + 1), 128 * k : 128 * (k + 1)].reshape(A, 16, 128)
            if p % 2 == 0:
                continue
            for e in RETURN_ORDER[p - 1 : p + 1]:
                there = rret.at[h, RETURN_ORDER.index(e), src * 4 + rcv % 4]
                if e == 0:
                    pltpu.make_async_copy(rslab.at[h, src, rcv], there, br.at[h, p // 2]).start()
            for o, (a, b) in sorted(zip(offsets, peers, strict=True), key=lambda p: -sum(min(v, 4 - v) for v in p[0][:3])):
                if o[0] in RETURN_ORDER[p - 1 : p + 1]:
                    pltpu.make_async_remote_copy(
                        src_ref=rslab.at[h, a, b],
                        dst_ref=rret.at[h, RETURN_ORDER.index(o[0]), src * 4 + rcv % 4],
                        send_sem=bs.at[h],
                        recv_sem=br.at[h, p // 2],
                        device_id=(a, b),
                        device_id_type=MESH,
                    ).start()
        return carry

    lax.fori_loop(0, 2, middle, 0)

    def gather(h, pair, turned):
        pltpu.make_async_copy(
            rret.at[h, pl.ds(2 * pair, 2)], rret.at[h, pl.ds(2 * pair, 2)], br.at[h, pair]
        ).wait()
        for i in range(8):
            v = rret[h, 2 * pair + i // 4, 8 * (i % 4) : 8 * (i % 4 + 1)]
            gath[256 * i : 256 * (i + 1), :] = v.reshape(256, 128).astype(F32)

        def turn(j, carry):
            w = gath[pl.ds(j, 128, stride=16), :].astype(BF)
            turned[pl.ds(pl.multiple_of(j * 128, 128), 128), 128 * pair : 128 * (pair + 1)] = nt(
                eye[0:128, 0:128], w
            ).astype(BF)
            return carry

        lax.fori_loop(0, 16, turn, 0, unroll=16)

    gather(0, 0, early)
    gather(0, 1, early)

    def first_half(i, carry):
        at = pl.ds(pl.multiple_of(i * 256, 256), 256)
        total[at, :] = nn(early[at, :], inv_early[...])
        return carry

    lax.fori_loop(0, 8, first_half, 0, unroll=4)
    gather(1, 0, late)
    gather(1, 1, late)

    whole = pl.ds(0, DEV - 1)
    for h in range(2):
        pltpu.make_async_copy(slab.at[h, whole], slab.at[h, whole], fs.at[h]).wait()
        pltpu.make_async_copy(slab.at[h, whole], slab.at[h, whole], bs.at[h]).wait()


def finish(total, late, inv_late, out, done, sem):
    copies = []
    for i in range(8):
        at = slice(256 * i, 256 * (i + 1))
        o = (total[at, :] + nn(late[at, :], inv_late[...])).astype(BF).reshape(2, 4, 32, NT)
        for jj in range(2):
            done[:, 2 * i + jj] = o[jj]
        copies.append(pltpu.make_async_copy(done.at[:, pl.ds(2 * i, 2)], out.at[:, pl.ds(2 * i, 2)], sem.at[i]))
        copies[-1].start()
    for copy in copies:
        copy.wait()


def local(records, surface_operator):
    forward, inverse = tables()
    packed = np.concatenate([forward, inverse, swap_matrix(), np.eye(256, 512, dtype=np.float32)])
    packed = jnp.asarray(packed).astype(BF)
    vmem = pl.BlockSpec(memory_space=pltpu.VMEM)
    total, late, inv_late = pl.pallas_call(
        kernel,
        name="multiples",
        out_shape=[
            jax.ShapeDtypeStruct((2048, NT), F32),
            jax.ShapeDtypeStruct((2048, NF), BF),
            jax.ShapeDtypeStruct((NF, NT), BF),
        ],
        in_specs=[pl.BlockSpec(memory_space=pl.ANY)] * 3,
        out_specs=[vmem] * 3,
        scratch_shapes=[
            pltpu.VMEM((64, 32, NT), BF),
            pltpu.VMEM((2 * NF, NT), BF),
            pltpu.VMEM((NF, NT), BF),
            pltpu.VMEM((256, 256), BF),
            pltpu.VMEM((512, 512), BF),
            pltpu.SMEM((2, NF), F32),
            pltpu.VMEM((2, 2048, 128), F32),
            pltpu.VMEM((2, DEV, 2, 16, 128), BF),
            pltpu.VMEM((2, A, B, 2, 16, 128), BF),
            pltpu.VMEM((2, A, 4, 16, 512), BF),
            pltpu.VMEM((512, 1024), BF),
            pltpu.VMEM((1024, 1024), BF),
            pltpu.VMEM((1024, 1024), BF),
            pltpu.VMEM((2, A, B, 2, 16, 128), BF),
            pltpu.VMEM((2, 4, 32, 2, 16, 128), BF),
            pltpu.VMEM((2048, 128), F32),
            pltpu.VMEM((2048, NF), BF),
            pltpu.SemaphoreType.DMA((2,)),
            pltpu.SemaphoreType.DMA((2,)),
            pltpu.SemaphoreType.DMA((2,)),
            pltpu.SemaphoreType.DMA((2, 2)),
            pltpu.SemaphoreType.DMA((4,)),
            pltpu.SemaphoreType.DMA((3,)),
        ],
        compiler_params=pltpu.CompilerParams(
            collective_id=0, has_side_effects=True, vmem_limit_bytes=40 * 1024 * 1024
        ),
    )(*[pltpu.with_memory_space_constraint(v, pltpu.HBM) for v in (records, packed, surface_operator.T)])
    multiples = pl.pallas_call(
        finish,
        name="finish",
        out_shape=jax.ShapeDtypeStruct((4, 16, 32, NT), BF),
        in_specs=[vmem] * 3,
        out_specs=pl.BlockSpec(memory_space=pl.ANY),
        scratch_shapes=[pltpu.VMEM((4, 16, 32, NT), BF), pltpu.SemaphoreType.DMA((8,))],
        compiler_params=pltpu.CompilerParams(vmem_limit_bytes=16 * 1024 * 1024),
    )(total, late, inv_late)
    return multiples.reshape(64, 32, NT)


def solution(mesh):
    placed = (P("src", "rcv", None), P())
    return jax.shard_map(
        local, mesh=mesh, in_specs=placed, out_specs=P("src", "rcv", None), check_vma=False
    )
```

```python
import math

import jax
import jax.numpy as jnp
import numpy as np
from jax import lax
from jax.experimental import pallas as pl
from jax.experimental.pallas import tpu as pltpu
from jax.sharding import PartitionSpec as P

MESH = pl.DeviceIdType.MESH
BF = jnp.bfloat16
F32 = jnp.float32
NS = 512
NT = 512
NF = 256
DEV = 128
A = 8
B = 16


def tables():
    f = np.arange(NF)[:, None]
    t = np.arange(NT)[None, :]
    angle = ((f * t) % NT).astype(np.float32) * np.float32(2.0 * math.pi / NT)
    norm = np.float32(1.0 / math.sqrt(NT))
    cosine, sine = np.cos(angle) * norm, np.sin(angle) * norm
    weight = np.where(f == 0, 1.0, 2.0).astype(np.float32)
    forward = np.stack([cosine, -sine], axis=1).reshape(DEV, 2, 2, NT)
    inverse = np.stack([weight * cosine, -weight * sine], axis=1).reshape(DEV, 2, 2, NT)
    forward = forward.transpose(1, 2, 0, 3).reshape(2 * NF, NT)
    inverse = inverse.reshape(A, 4, 4, 2, 2, NT).transpose(1, 3, 0, 2, 4, 5).reshape(2 * NF, NT)
    return forward, inverse


def swap_matrix():
    m = np.zeros((4, 4, 32, 4, 4, 32), np.float32)
    for x in range(4):
        for y in range(4):
            for r in range(32):
                m[x, y, r, y, x, r] = 1.0
    return m.reshape(512, 512)


def mixed_offsets():
    offsets = [(x, y, z, c) for x in range(4) for y in range(4) for z in range(4) for c in range(2)][1:]
    return [offsets[i] for i in np.random.RandomState(1).permutation(len(offsets))]


RETURN_ORDER = (2, 1, 0, 3)


def nt(left, right):
    return lax.dot_general(left, right, (((1,), (1,)), ((), ())), preferred_element_type=F32)


def nn(left, right):
    return jnp.dot(left, right, preferred_element_type=F32)


def kernel(
    rec_in, tab_in, coef_in, total, late, inv_late,
    rec, fwd, inv_early, eye, swap, coef,
    wide, slab, rbuf, spec, q_a, b_one, b_two, rslab, rret, gath, early,
    fs, fr, bs, br, loaded, filled,
):
    def tab(i):
        return tab_in.at[pl.ds(512 * i, 512)]

    loads = [
        pltpu.make_async_copy(here, there, loaded.at[i])
        for i, (here, there) in enumerate(
            [(tab(0), fwd), (tab(2), swap), (tab_in.at[pl.ds(1536, 256), pl.ds(0, 256)], eye), (coef_in, coef)]
        )
    ]
    loads[0].start()
    traces_in = pltpu.make_async_copy(rec_in, rec, filled.at[0])
    traces_in.start()
    src, rcv = lax.axis_index("src"), lax.axis_index("rcv")
    me = src * B + rcv
    z, y_hi = src // 2, src % 2
    x, y_lo, core = rcv // 4, (rcv // 2) % 2, rcv % 2
    y = y_hi * 2 + y_lo

    barrier = pltpu.get_barrier_semaphore()

    xs = [lax.rem(x + d, 4) * 4 for d in range(4)]
    ys = [lax.rem(y + d, 4) for d in range(4)]
    y_s = [v // 2 for v in ys]
    y_r = [(v % 2) * 2 for v in ys]
    zs = [lax.rem(z + d, 4) * 2 for d in range(4)]
    cs = [lax.rem(core + d, 2) for d in range(2)]
    offsets = mixed_offsets()
    peers = [(zs[o[2]] + y_s[o[1]], xs[o[0]] + y_r[o[1]] + cs[o[3]]) for o in offsets]
    for _, to in sorted(zip(offsets, peers, strict=True), key=lambda p: -sum(min(v, 4 - v) for v in p[0][:3])):
        pl.semaphore_signal(barrier, inc=1, device_id=to, device_id_type=MESH)
    for load in loads[1:]:
        load.start()
    loads[0].wait()
    traces_in.wait()

    def dft(h):
        def step(pair, carry):
            j = 2 * pair
            traces = jnp.concatenate([rec[16 * q + j + jj] for jj in range(2) for q in range(4)], axis=0)
            o = nt(fwd[256 * h : 256 * (h + 1)], traces)
            for c in range(2):
                for jj in range(2):
                    wide[c, pl.ds(j + jj, DEV, stride=16), :] = o[
                        128 * c : 128 * (c + 1), 128 * jj : 128 * (jj + 1)
                    ]
            return carry

        lax.fori_loop(0, 8, step, 0, unroll=8)

        def pack(i, carry):
            for c in range(2):
                v = wide[c, pl.ds(i * 256, 256), :]
                slab[h, pl.ds(i * 16, 16), c] = v.astype(BF).reshape(16, 16, 128)
            return carry

        lax.fori_loop(0, 8, pack, 0, unroll=4)

    def forward_sends(h):
        mine = pltpu.make_async_copy(slab.at[h, me], rbuf.at[h, src, rcv], fr.at[h])
        mine.start()
        for _, (a, b) in sorted(zip(offsets, peers, strict=True), key=lambda p: -sum(min(v, 4 - v) for v in p[0][:3])) if h == 0 else zip(offsets, peers, strict=True):
            pltpu.make_async_remote_copy(
                src_ref=slab.at[h, a * B + b],
                dst_ref=rbuf.at[h, src, rcv],
                send_sem=fs.at[h],
                recv_sem=fr.at[h],
                device_id=(a, b),
                device_id_type=MESH,
            ).start()

    dft(0)
    pl.semaphore_wait(barrier, DEV - 1)
    forward_sends(0)
    dft(1)
    forward_sends(1)
    for h in range(2):
        for p, d in enumerate(RETURN_ORDER):
            at = pl.multiple_of((lax.rem(x + 4 - d, 4) * 2 + h) * 64 + 512, 64)
            pltpu.make_async_copy(
                tab_in.at[pl.ds(at, 64)], (inv_late if h else inv_early).at[pl.ds(64 * p, 64)], filled.at[1 + h]
            ).start()
    for load in loads[1:]:
        load.wait()
    pltpu.make_async_copy(inv_early, inv_early, filled.at[1]).wait()
    pltpu.make_async_copy(inv_late, inv_late, filled.at[2]).wait()

    norm = 1.0 / math.sqrt(NS)

    def middle(h, carry):
        pltpu.make_async_copy(rbuf.at[h], rbuf.at[h], fr.at[h]).wait()
        for c in range(2):
            piece = jnp.concatenate(
                [
                    jnp.concatenate([rbuf[h, :, 4 * bb + k, c].reshape(128, 128) for k in range(4)], axis=1)
                    for bb in range(4)
                ],
                axis=0,
            )
            s = nn(piece, swap[...]).astype(BF)
            for bb in range(4):
                for q in range(4):
                    spec[c, :, q, :, 128 * bb : 128 * (bb + 1)] = s[
                        128 * bb : 128 * (bb + 1), 128 * q : 128 * (q + 1)
                    ].reshape(A, 16, 128)
        for c in range(2):
            for m in range(2):
                for n in range(2):
                    turned_s = nt(eye[...], spec[c, 4 * n : 4 * n + 4, :, :, 256 * m : 256 * (m + 1)].reshape(256, 256))
                    plain = spec[c, 4 * m : 4 * m + 4, :, :, 256 * n : 256 * (n + 1)].reshape(256, 256)
                    q = (0.5 * (plain.astype(F32) + turned_s)).astype(BF)
                    rows, cols = slice(256 * m, 256 * (m + 1)), slice(256 * n, 256 * (n + 1))
                    low, right = slice(512 + 256 * m, 768 + 256 * m), slice(512 + 256 * n, 768 + 256 * n)
                    if c == 0:
                        q_a[rows, cols] = q
                        b_one[rows, cols] = q
                        b_one[low, right] = q
                    else:
                        q_a[rows, right] = q
                        b_one[rows, right] = q
                        b_one[low, cols] = -q
        at = 2 * me + h
        k_r, k_i = coef[0, at] * norm, coef[1, at] * norm

        def scaled(o):
            half = o.shape[1] // 2
            r, i = o[:, :half], o[:, half:]
            return k_r * r - k_i * i, k_r * i + k_i * r

        def product(source, target):
            def rows_of(m, carry2):
                at_m = pl.multiple_of(m * 256, 256)
                r, i = scaled(nn(q_a[pl.ds(at_m, 256), :], source[...]))
                r, i = r.astype(BF), i.astype(BF)
                target[pl.ds(at_m, 256), 0:512] = r
                target[pl.ds(at_m, 256), 512:1024] = i
                target[pl.ds(at_m + 512, 256), 0:512] = -i
                target[pl.ds(at_m + 512, 256), 512:1024] = r
                return carry2

            lax.fori_loop(0, 2, rows_of, 0)

        product(b_one, b_two)
        product(b_two, b_one)

        for p, d in enumerate(RETURN_ORDER):
            bb = lax.rem(x + d, 4)
            cols = [pl.ds(pl.multiple_of(512 * c + 128 * bb, 128), 128) for c in range(2)]
            third = scaled(nn(q_a[...], jnp.concatenate([b_one[:, cols[0]], b_one[:, cols[1]]], axis=1)))
            pieces = []
            for c in range(2):
                summed = b_two[0:512, cols[c]].astype(F32) + b_one[0:512, cols[c]].astype(F32) + third[c]
                summed = summed.astype(BF).reshape(A, 4, 16, 128)
                pieces.append(jnp.concatenate([summed[:, q].reshape(128, 128) for q in range(4)], axis=1))
            s = nn(jnp.concatenate(pieces, axis=0), swap[...]).astype(BF)
            for c in range(2):
                for k in range(4):
                    rslab[h, :, 4 * bb + k, c] = s[128 * c : 128 * (c + 1), 128 * k : 128 * (k + 1)].reshape(A, 16, 128)
            if p % 2 == 0:
                continue
            for e in RETURN_ORDER[p - 1 : p + 1]:
                there = rret.at[h, RETURN_ORDER.index(e), src * 4 + rcv % 4]
                if e == 0:
                    pltpu.make_async_copy(rslab.at[h, src, rcv], there, br.at[h, p // 2]).start()
            for o, (a, b) in sorted(zip(offsets, peers, strict=True), key=lambda p: -sum(min(v, 4 - v) for v in p[0][:3])):
                if o[0] in RETURN_ORDER[p - 1 : p + 1]:
                    pltpu.make_async_remote_copy(
                        src_ref=rslab.at[h, a, b],
                        dst_ref=rret.at[h, RETURN_ORDER.index(o[0]), src * 4 + rcv % 4],
                        send_sem=bs.at[h],
                        recv_sem=br.at[h, p // 2],
                        device_id=(a, b),
                        device_id_type=MESH,
                    ).start()
        return carry

    lax.fori_loop(0, 2, middle, 0)

    def gather(h, pair, turned):
        pltpu.make_async_copy(
            rret.at[h, pl.ds(2 * pair, 2)], rret.at[h, pl.ds(2 * pair, 2)], br.at[h, pair]
        ).wait()
        for i in range(8):
            v = rret[h, 2 * pair + i // 4, 8 * (i % 4) : 8 * (i % 4 + 1)]
            gath[256 * i : 256 * (i + 1), :] = v.reshape(256, 128).astype(F32)

        def turn(j, carry):
            w = gath[pl.ds(j, 128, stride=16), :].astype(BF)
            turned[pl.ds(pl.multiple_of(j * 128, 128), 128), 128 * pair : 128 * (pair + 1)] = nt(
                eye[0:128, 0:128], w
            ).astype(BF)
            return carry

        lax.fori_loop(0, 16, turn, 0, unroll=16)

    gather(0, 0, early)
    gather(0, 1, early)

    def first_half(i, carry):
        at = pl.ds(pl.multiple_of(i * 256, 256), 256)
        total[at, :] = nn(early[at, :], inv_early[...])
        return carry

    lax.fori_loop(0, 8, first_half, 0, unroll=8)
    gather(1, 0, late)
    gather(1, 1, late)

    whole = pl.ds(0, DEV - 1)
    for h in range(2):
        pltpu.make_async_copy(slab.at[h, whole], slab.at[h, whole], fs.at[h]).wait()
        pltpu.make_async_copy(slab.at[h, whole], slab.at[h, whole], bs.at[h]).wait()


def finish(total, late, inv_late, out, done, sem):
    copies = []
    for i in range(16):
        at = slice(128 * i, 128 * (i + 1))
        done[:, i] = (total[at, :] + nn(late[at, :], inv_late[...])).astype(BF).reshape(4, 32, NT)
        copies.append(pltpu.make_async_copy(done.at[:, i], out.at[:, i], sem.at[i]))
        copies[-1].start()
    for copy in copies:
        copy.wait()


def local(records, surface_operator):
    forward, inverse = tables()
    packed = np.concatenate([forward, inverse, swap_matrix(), np.eye(256, 512, dtype=np.float32)])
    packed = jnp.asarray(packed).astype(BF)
    vmem = pl.BlockSpec(memory_space=pltpu.VMEM)
    total, late, inv_late = pl.pallas_call(
        kernel,
        name="multiples",
        out_shape=[
            jax.ShapeDtypeStruct((2048, NT), F32),
            jax.ShapeDtypeStruct((2048, NF), BF),
            jax.ShapeDtypeStruct((NF, NT), BF),
        ],
        in_specs=[pl.BlockSpec(memory_space=pl.ANY)] * 3,
        out_specs=[vmem] * 3,
        scratch_shapes=[
            pltpu.VMEM((64, 32, NT), BF),
            pltpu.VMEM((2 * NF, NT), BF),
            pltpu.VMEM((NF, NT), BF),
            pltpu.VMEM((256, 256), BF),
            pltpu.VMEM((512, 512), BF),
            pltpu.SMEM((2, NF), F32),
            pltpu.VMEM((2, 2048, 128), F32),
            pltpu.VMEM((2, DEV, 2, 16, 128), BF),
            pltpu.VMEM((2, A, B, 2, 16, 128), BF),
            pltpu.VMEM((2, A, 4, 16, 512), BF),
            pltpu.VMEM((512, 1024), BF),
            pltpu.VMEM((1024, 1024), BF),
            pltpu.VMEM((1024, 1024), BF),
            pltpu.VMEM((2, A, B, 2, 16, 128), BF),
            pltpu.VMEM((2, 4, 32, 2, 16, 128), BF),
            pltpu.VMEM((2048, 128), F32),
            pltpu.VMEM((2048, NF), BF),
            pltpu.SemaphoreType.DMA((2,)),
            pltpu.SemaphoreType.DMA((2,)),
            pltpu.SemaphoreType.DMA((2,)),
            pltpu.SemaphoreType.DMA((2, 2)),
            pltpu.SemaphoreType.DMA((4,)),
            pltpu.SemaphoreType.DMA((3,)),
        ],
        compiler_params=pltpu.CompilerParams(
            collective_id=0, has_side_effects=True, vmem_limit_bytes=40 * 1024 * 1024
        ),
    )(*[pltpu.with_memory_space_constraint(v, pltpu.HBM) for v in (records, packed, surface_operator.T)])
    multiples = pl.pallas_call(
        finish,
        name="finish",
        out_shape=jax.ShapeDtypeStruct((4, 16, 32, NT), BF),
        in_specs=[vmem] * 3,
        out_specs=pl.BlockSpec(memory_space=pl.ANY),
        scratch_shapes=[pltpu.VMEM((4, 16, 32, NT), BF), pltpu.SemaphoreType.DMA((16,))],
        compiler_params=pltpu.CompilerParams(vmem_limit_bytes=16 * 1024 * 1024),
    )(total, late, inv_late)
    return multiples.reshape(64, 32, NT)


def solution(mesh):
    placed = (P("src", "rcv", None), P())
    return jax.shard_map(
        local, mesh=mesh, in_specs=placed, out_specs=P("src", "rcv", None), check_vma=False
    )
```
